256 devices in a mesh: sec: 8 (over y, core), dom: 32 (over x, z).
Axes of the slice: x: 4, y: 4, z: 8, core: 2. Of those that a mesh axis runs over, the one named last changes fastest.
Arguments:
- flow_state: bfloat16 [270, 262144], P(None, ('sec', 'dom')), may hold values from -6 to 6
- base_geometry: float32 [4, 262144], P(None, ('sec', 'dom')), may hold values from 0.5 to 2
- anchor_weight: float32 [262144], P(('sec', 'dom')), may hold values from 0 to 1.5
- wall_anchor: int32 [262144], P(('sec', 'dom')), may hold values from 0 to 262143
- face_nbr: int32 [6, 262144], P(None, ('sec', 'dom')), may hold values from 0 to 1151, as said below
- volume_ops: bfloat16 [4, 270, 270], replicated, may hold values from -0.375 to 0.375
- lift_ops: bfloat16 [6, 270, 90], replicated, may hold values from -0.625 to 0.625
- face_jac: bfloat16 [6, 2, 5, 5], replicated, may hold values from -2.5 to 2.5
- wall_load: float32 [3, 2048, 128], P(None, ('sec', 'dom')), may hold values from -6 to 6
- wall_stiff: float32 [3, 2048, 128], P(None, ('sec', 'dom')), may hold values from 0.01 to 0.3
Outputs:
- flow_residual: bfloat16 [270, 262144], P(None, ('sec', 'dom'))
- wall_disp: float32 [3, 2048, 128], P(None, ('sec', 'dom'))
The draws below stay inside these ranges and needn't reach their ends.
Inputs may be any that keep to these rules, and one draw needn't show every extreme that they name: `face_nbr`: for faces 0 to 3 a value v >= 1024 names element v - 1024 (below 128) of the device one step lower (faces 0 and 2) or higher (faces 1 and 3), cyclically, along dom (faces 0 and 1) or sec (faces 2 and 3); a smaller value names an element of the element's own device. Faces 4 and 5 always name an element of the own device.
All inputs are finite; a program needn't handle non-finite values.
Results may differ from the reference program's by a relative error of at most 0.0046.
Values may be sent and summed in bfloat16 or wider, within the bound.
A program may use at most 320 MiB of HBM per device.

```python
import math
import jax
import jax.numpy as jnp
from jax import lax

NV = 5
NQ = 270
NF = 90
E_DEV = 1024
HB = 128
NE = 262144
WB = 128
WA = 2048
NW = 262144
ITERS = 8
N_SEC = 8
N_DOM = 32


def draw_face_nbr(key, part):
    first = jax.random.fold_in(key, 11)
    second = jax.random.fold_in(key, 12)
    third = jax.random.fold_in(key, 13)
    local_pick = jax.random.randint(first, (6, NE), 0, E_DEV, dtype=jnp.int32)
    remote_pick = jax.random.randint(second, (6, NE), 0, HB, dtype=jnp.int32) + E_DEV
    remote_flag = jax.random.randint(third, (6, NE), 0, 2, dtype=jnp.int32) == 1
    crossing = jnp.arange(6, dtype=jnp.int32)[:, None] < 4
    neighbours = jnp.where(remote_flag & crossing, remote_pick, local_pick)
    neighbours = neighbours.at[0, 0].set(E_DEV + HB - 1)
    neighbours = neighbours.at[4, 0].set(0)
    return neighbours.astype(jnp.int32)


def plant(result, rng, least, top_value):
    extent = result.shape
    place = [jax.random.randint(jax.random.fold_in(rng, axis), (), 0, extent[axis]) for axis in range(len(extent))]
    result = result.at[tuple(place)].set(least)
    longest = extent.index(max(extent))
    place[longest] = (place[longest] + 1) % extent[longest]
    return result.at[tuple(place)].set(top_value)


def levels(rng, shape, split, smallest, largest):
    factor_of, own = 1.0, jax.random.fold_in(rng, 6)
    for position, blocks in split:
        draws = jnp.exp(jax.random.uniform(jax.random.fold_in(own, position), (blocks,), jnp.float32, smallest / len(split), largest / len(split)))
        factor_of = factor_of * jnp.repeat(draws, shape[position] // blocks).reshape([-1 if axis == position else 1 for axis in range(len(shape))])
    return factor_of


def centred(key, shape, spread, reach, split=(), kind=jnp.bfloat16):
    drawn = jax.random.normal(key, shape, jnp.float32) * spread
    if len(split) > 0:
        drawn = levels(key, shape, split, -0.22, 0.18) * drawn
    return jnp.clip(drawn, min=-reach, max=reach).astype(kind)


def setup_inputs(seed: int = 0) -> dict:
    seeds = jax.random.split(jax.random.key(seed), 11)
    flow_state = centred(seeds[0], (NQ, NE), 1.0, 6.0, ((1, 256),))
    base_geometry = jnp.clip(jnp.exp(math.log(2.0) - 1.3862944 * jax.random.uniform(seeds[1], (4, NE), jnp.float32) ** levels(seeds[1], (4, NE), ((1, 256),), -0.2, 0.2)), 0.5, 2.0)
    anchor_weight = jnp.clip(1.5 * jax.random.uniform(seeds[2], (NE,), jnp.float32) ** levels(seeds[2], (NE,), ((0, 256),), -0.2, 0.2), 0.0, 1.5)
    wall_anchor = plant(jax.random.randint(seeds[3], (NE,), 0, NW), jax.random.fold_in(seeds[3], 1), 0, NW - 1).astype(jnp.int32)
    face_nbr = draw_face_nbr(jax.random.fold_in(seeds[10], 71), 0)
    volume_ops = centred(seeds[5], (4, NQ, NQ), NQ ** -0.5, 0.375)
    lift_ops = centred(seeds[6], (6, NQ, NF), NF ** -0.5, 0.625)
    face_jac = centred(seeds[7], (6, 2, NV, NV), NV ** -0.5, 2.5)
    wall_load = centred(seeds[8], (3, WA, WB), 1.0, 6.0, ((1, 256),), jnp.float32)
    wall_stiff = jnp.clip(jnp.exp(math.log(0.3) - 3.4011974 * jax.random.uniform(seeds[9], (3, WA, WB), jnp.float32) ** levels(seeds[9], (3, WA, WB), ((1, 256),), -0.2, 0.2)), 0.01, 0.3)
    return dict(flow_state=flow_state, base_geometry=base_geometry, anchor_weight=anchor_weight, wall_anchor=wall_anchor, face_nbr=face_nbr, volume_ops=volume_ops, lift_ops=lift_ops, face_jac=face_jac, wall_load=wall_load, wall_stiff=wall_stiff)


def wall_operator(field, stiffness):
    padded = jnp.pad(field, ((0, 0), (1, 1), (1, 1)))
    beside = padded[:, 2:, 1:-1] + padded[:, :-2, 1:-1] + padded[:, 1:-1, 2:] + padded[:, 1:-1, :-2]
    return (4.0 + stiffness) * field - beside


def face_trace(values, face):
    shaped = values.reshape(NV, 2, 3, 3, 3, values.shape[1])
    picked = lax.index_in_dim(shaped, 0 if face % 2 == 0 else 2, 2 + face // 2, keepdims=False)
    return picked.reshape(NV * 18, values.shape[1])


def residual_block(state, geometry, neighbours, remotes, volume_ops, lift_ops, face_jac):
    summed = jnp.zeros(state.shape, jnp.float32)
    for direction in range(4):
        summed = summed + geometry[direction][None, :] * jnp.dot(volume_ops[direction], state, preferred_element_type=jnp.float32)
    identity = jnp.eye(18, dtype=jnp.bfloat16)
    for face in range(6):
        own_trace = face_trace(state, face)
        opposite = face_trace(state, face ^ 1)
        if face < 4:
            candidates = jnp.concatenate([opposite, remotes[face]], axis=1)
        else:
            candidates = opposite
        neighbour_trace = jnp.take(candidates, neighbours[face], axis=1)
        own_jac = jnp.kron(face_jac[face, 0], identity)
        other_jac = jnp.kron(face_jac[face, 1], identity)
        face_flux = geometry[face // 2][None, :] * (jnp.dot(own_jac, own_trace, preferred_element_type=jnp.float32) + jnp.dot(other_jac, neighbour_trace, preferred_element_type=jnp.float32))
        face_flux = face_flux.astype(jnp.bfloat16)
        summed = summed + jnp.dot(lift_ops[face], face_flux, preferred_element_type=jnp.float32)
    return summed.astype(jnp.bfloat16)


def reference(flow_state, base_geometry, anchor_weight, wall_anchor, face_nbr, volume_ops, lift_ops, face_jac, wall_load, wall_stiff):
    wall_disp = jnp.zeros_like(wall_load)
    resid = wall_load
    search = wall_load
    norm_now = jnp.sum(resid * resid)
    for iteration in range(ITERS):
        image = wall_operator(search, wall_stiff)
        step_size = norm_now / jnp.sum(search * image)
        wall_disp = wall_disp + step_size * search
        resid = resid - step_size * image
        norm_next = jnp.sum(resid * resid)
        search = resid + (norm_next / norm_now) * search
        norm_now = norm_next
    flattened = wall_disp.reshape(3, WA * WB)
    disp_at = jnp.take(flattened, wall_anchor, axis=1)
    geometry = jnp.concatenate([base_geometry[:3] * jnp.exp(anchor_weight[None, :] * disp_at), base_geometry[3:]], axis=0)

    def block_of(array, which):
        return lax.dynamic_slice_in_dim(array, (which * E_DEV).astype(jnp.int32), E_DEV, 1)

    def one_device(device):
        sec_pos = device // N_DOM
        dom_pos = device % N_DOM
        dom_low = sec_pos * N_DOM + (dom_pos - 1) % N_DOM
        dom_high = sec_pos * N_DOM + (dom_pos + 1) % N_DOM
        sec_low = ((sec_pos - 1) % N_SEC) * N_DOM + dom_pos
        sec_high = ((sec_pos + 1) % N_SEC) * N_DOM + dom_pos
        remotes = [
            face_trace(block_of(flow_state, dom_low)[:, :HB], 1),
            face_trace(block_of(flow_state, dom_high)[:, :HB], 0),
            face_trace(block_of(flow_state, sec_low)[:, :HB], 3),
            face_trace(block_of(flow_state, sec_high)[:, :HB], 2),
        ]
        return residual_block(block_of(flow_state, device), block_of(geometry, device), block_of(face_nbr, device), remotes, volume_ops, lift_ops, face_jac)

    blocks = lax.map(one_device, jnp.arange(N_SEC * N_DOM, dtype=jnp.int32))
    flow_residual = jnp.moveaxis(blocks, 0, 1).reshape(NQ, NE)
    return flow_residual, wall_disp
```

```python
import functools

import jax
import jax.numpy as jnp
import numpy as np
from jax import lax
from jax.experimental import pallas as pl
from jax.experimental.pallas import tpu as pltpu
from jax.sharding import PartitionSpec as P

MESH = pl.DeviceIdType.MESH
ITERS = 8
NQ = 270
NF = 90
NE = 1024
HB = 128
NY, NC, NX, NZ = 4, 2, 4, 8
SIZE = {"y": NY, "x": NX, "z": NZ}
ORDERS = (("z", "x", "y"), ("x", "y", "z"), ("y", "z", "x"))
STEPS = sum(SIZE.values()) // 2
F32 = jnp.float32
BF16 = jnp.bfloat16


def selection():
    index = np.arange(NQ).reshape(5, 2, 3, 3, 3)
    rows = np.zeros((6, 128, NQ), np.float32)
    for face in range(6):
        picked = np.take(index, 0 if face % 2 == 0 else 2, axis=2 + face // 2).reshape(-1)
        rows[face, np.arange(NF), picked] = 1.0
    return rows


def expansion():
    spread = np.zeros((128, 5), np.float32)
    spread[np.arange(NF), np.arange(NF) // 18] = 1.0
    same = np.zeros((128, 128), np.float32)
    inside = np.arange(NF)
    same[:NF, :NF] = inside[:, None] % 18 == inside[None, :] % 18
    return spread, same


def coordinates():
    sec, dom = lax.axis_index("sec"), lax.axis_index("dom")
    return {"y": sec // NC, "core": sec % NC, "x": dom // NZ, "z": dom % NZ}


def device(place):
    return (place["y"] * NC + place["core"], place["x"] * NZ + place["z"])


def moved(place, axis, by):
    size = SIZE[axis]
    return dict(place, **{axis: (place[axis] + by + size) % size})


class Gather:
    def __init__(self, color, here, wall, send, recv, pass_send, pass_recv):
        self.color, self.here, self.wall = color, here, wall
        self.send, self.recv = send, recv
        self.pass_send, self.pass_recv = pass_send, pass_recv
        self.plan = []
        for stage, axis in enumerate(ORDERS[color]):
            for step in range(SIZE[axis] // 2):
                self.plan.append((stage, axis, step))
        self.passed = []

    def block(self, stage, axis, at, half):
        order = ORDERS[self.color]
        index = {}
        for name in "yxz":
            if name in order[:stage]:
                index[name] = slice(None)
            elif name == axis:
                index[name] = at
            else:
                index[name] = self.here[name]
        which = slice(None) if half is None else half
        return self.wall.at[self.color, which, index["y"], self.here["core"], index["x"], index["z"]]

    def copies(self, number):
        stage, axis, step = self.plan[number]
        size = SIZE[axis]
        made = []
        for way, sign in enumerate((1, -1)):
            half = None if step < size // 2 - 1 else way
            at = (self.here[axis] - sign * step + size) % size
            source = self.block(stage, axis, at, half)
            slot = (self.color * STEPS + number) * 2 + way
            made.append(
                pltpu.make_async_remote_copy(
                    src_ref=source,
                    dst_ref=source,
                    send_sem=self.send.at[slot],
                    recv_sem=self.recv.at[slot],
                    device_id=device(moved(self.here, axis, sign)),
                    device_id_type=MESH,
                )
            )
        return made

    def hand_over(self, at):
        axis = ORDERS[self.color][2]
        slot = self.color * NZ + len(self.passed)
        source = self.block(2, axis, at, None)
        copy = pltpu.make_async_remote_copy(
            src_ref=source,
            dst_ref=source,
            send_sem=self.pass_send.at[slot],
            recv_sem=self.pass_recv.at[slot],
            device_id=device(dict(self.here, core=1 - self.here["core"])),
            device_id_type=MESH,
        )
        copy.start()
        self.passed.append(copy)

    def advance(self, number):
        if number > 0:
            stage, axis, step = self.plan[number - 1]
            for copy in self.copies(number - 1):
                copy.wait_recv()
            if stage == 2:
                size = SIZE[axis]
                self.hand_over((self.here[axis] - step - 1 + size) % size)
                if step < size // 2 - 1:
                    self.hand_over((self.here[axis] + step + 1) % size)
        if number < STEPS:
            stage, axis, step = self.plan[number]
            for copy in self.copies(number):
                copy.start()
            if stage == 2 and step == 0:
                self.hand_over(self.here[axis])

    def finish(self):
        for number in range(STEPS):
            for copy in self.copies(number):
                copy.wait_send()
        for copy in self.passed:
            copy.wait()


def exchange_kernel(load, stiff, flow, wall, heads, send, recv, pass_send, pass_recv, head_send, head_recv, own_sem):
    here = coordinates()
    sec, dom = lax.axis_index("sec"), lax.axis_index("dom")
    n_sec, n_dom = NY * NC, NX * NZ
    sides = [
        (sec, (dom + 1) % n_dom),
        (sec, (dom + n_dom - 1) % n_dom),
        ((sec + 1) % n_sec, dom),
        ((sec + n_sec - 1) % n_sec, dom),
    ]
    peers = list(sides)
    for axis in "yxz":
        peers.append(device(moved(here, axis, 1)))
        peers.append(device(moved(here, axis, -1)))
    peers.append(device(dict(here, core=1 - here["core"])))
    own = wall.at[:, :, here["y"], here["core"], here["x"], here["z"]]
    mine = [
        pltpu.make_async_copy(load, own.at[:, 0], own_sem.at[0]),
        pltpu.make_async_copy(stiff, own.at[:, 1], own_sem.at[1]),
    ]
    for copy in mine:
        copy.start()
    barrier = pltpu.get_barrier_semaphore()
    for peer in peers:
        pl.semaphore_signal(barrier, inc=1, device_id=peer, device_id_type=MESH)
    pl.semaphore_wait(barrier, len(peers))
    for copy in mine:
        copy.wait()
    gathers = [Gather(color, here, wall, send, recv, pass_send, pass_recv) for color in range(3)]
    head_copies = []
    for number in range(STEPS + 1):
        for gather in gathers:
            gather.advance(number)
        if number == 0:
            for face, peer in enumerate(sides):
                copy = pltpu.make_async_remote_copy(
                    src_ref=flow.at[:, pl.ds(0, HB)],
                    dst_ref=heads.at[face],
                    send_sem=head_send.at[face],
                    recv_sem=head_recv.at[face],
                    device_id=peer,
                    device_id_type=MESH,
                )
                copy.start()
                head_copies.append(copy)
    for copy in head_copies:
        copy.wait()
    for gather in gathers:
        gather.finish()


def exchange(wall_load, wall_stiff, flow_state):
    vmem = pl.BlockSpec(memory_space=pltpu.VMEM)
    slots = 3 * STEPS * 2
    return pl.pallas_call(
        exchange_kernel,
        out_shape=(
            jax.ShapeDtypeStruct((3, 2, NY, NC, NX, NZ, 8, 128), F32),
            jax.ShapeDtypeStruct((4, NQ, HB), BF16),
        ),
        in_specs=[vmem] * 3,
        out_specs=(vmem, vmem),
        scratch_shapes=[
            pltpu.SemaphoreType.DMA((slots,)),
            pltpu.SemaphoreType.DMA((slots,)),
            pltpu.SemaphoreType.DMA((3 * NZ,)),
            pltpu.SemaphoreType.DMA((3 * NZ,)),
            pltpu.SemaphoreType.DMA((4,)),
            pltpu.SemaphoreType.DMA((4,)),
            pltpu.SemaphoreType.DMA((2,)),
        ],
        compiler_params=pltpu.CompilerParams(
            collective_id=0, has_side_effects=True, vmem_limit_bytes=16 << 20
        ),
        name="exchange",
    )(wall_load, wall_stiff, flow_state)


def dot(a, b):
    return jnp.dot(a, b, preferred_element_type=F32)


def residual_parts(flow, heads, nbr, vol, lift, jac, sel, spread, same, products, jumps, lifts, cand, pair):
    state = flow[...]
    for direction in range(4):
        products[direction] = dot(vol[direction], state)
    lifts[...] = jnp.zeros_like(lifts)
    pair[...] = jnp.zeros_like(pair)
    row = lax.broadcasted_iota(jnp.int32, (256, 1), 0).astype(F32).astype(BF16)
    for face in range(6):
        lifts[:, pl.ds(face * 128, NF)] = lift[face]
        other = sel[face ^ 1]
        cand[:, pl.ds(0, NE)] = dot(other, state).astype(BF16)
        width = NE
        if face < 4:
            cand[:, pl.ds(NE, HB)] = dot(other, heads[face]).astype(BF16)
            width = NE + HB
        place = nbr[pl.ds(face, 1), :]
        total = jnp.zeros((128, NE), F32)
        for start in range(0, width, 256):
            size = min(256, width - start)
            key = jnp.where((place >= start) & (place < start + size), place - start, -1)
            key = key.astype(F32).astype(BF16)
            chosen = jnp.where(row[:size] == key, jnp.ones((), BF16), jnp.zeros((), BF16))
            total = total + dot(cand[:, pl.ds(start, size)], chosen)
        pair[pl.ds(0, 128), :] = dot(sel[face], state).astype(BF16)
        pair[pl.ds(128, 128), :] = total.astype(BF16)
        mixes = []
        for side in range(2):
            wide = dot(spread[...], jac[face, side]).astype(BF16)
            wide = lax.dot_general(wide, spread[...], (((1,), (1,)), ((), ())), preferred_element_type=F32)
            mixes.append((wide * same[...]).astype(BF16))
        jumps[pl.ds(face * 128, 128), :] = dot(mixes[0], pair[pl.ds(0, 128), :]) + dot(mixes[1], pair[pl.ds(128, 128), :])


def solve_wall(wall, disp, resid, search, image, diag):
    T = 256
    lane = lax.broadcasted_iota(jnp.int32, (8, 128), 1)
    not_first = (lane != 0).astype(F32)
    not_last = (lane != 127).astype(F32)
    sub = lax.broadcasted_iota(jnp.int32, (8, 128), 0)
    zero = jnp.zeros((8, 128), F32)

    def total(acc):
        return jnp.sum(jnp.sum(acc, axis=0, keepdims=True), axis=1, keepdims=True)

    def start(c, acc):
        def body(t, acc):
            b = wall[c, 0, pl.ds(t, 8, stride=T), :]
            k = wall[c, 1, pl.ds(t, 8, stride=T), :]
            resid[c * T + t] = b
            diag[c * T + t] = 4.0 + k
            return acc + b * b

        return lax.fori_loop(0, T, body, acc, unroll=8)

    acc = zero
    for c in range(3):
        acc = start(c, acc)
    norm_now = total(acc)
    U = 8
    ratio = None
    for iteration in range(ITERS):
        first, last = iteration == 0, iteration == ITERS - 1

        def direction(i):
            if first:
                return resid[i]
            return resid[i] + ratio_b * search[i]

        if not first:
            ratio_b = jnp.broadcast_to(ratio, (8, 128))
        acc = zero
        for c in range(3):
            base = c * T
            top = direction(base)
            bottom = direction(base + T - 1)
            before = jnp.where(sub == 0, 0.0, pltpu.roll(bottom, 1, 0))
            beyond = jnp.where(sub == 7, 0.0, pltpu.roll(top, 7, 0))

            def one(t, above, here, below, acc):
                i = base + t
                beside = above + below + pltpu.roll(here, 1, 1) * not_first + pltpu.roll(here, 127, 1) * not_last
                value = diag[i] * here - beside
                if not last:
                    image[i] = value
                if not first:
                    search[i] = here
                return acc + here * value

            def block(b, carry):
                above, here, acc = carry
                for u in range(U):
                    t = b * U + u
                    below = direction(base + t + 1)
                    acc = one(t, above, here, below, acc)
                    above, here = here, below
                return above, here, acc

            above, here, acc = lax.fori_loop(0, T // U - 1, block, (before, top, acc))
            for t in range(T - U, T):
                below = beyond if t == T - 1 else direction(base + t + 1)
                acc = one(t, above, here, below, acc)
                above, here = here, below
        step = norm_now / total(acc)
        step_b = jnp.broadcast_to(step, (8, 128))

        def update(b, acc):
            for u in range(U):
                i = b * U + u
                r = resid[i]
                if first:
                    p = r
                    search[i] = r
                    disp[i] = step_b * p
                else:
                    p = search[i]
                    disp[i] = disp[i] + step_b * p
                if not last:
                    r = r - step_b * image[i]
                    resid[i] = r
                    acc = acc + r * r
            return acc

        acc = lax.fori_loop(0, 3 * T // U, update, zero)
        if not last:
            norm_next = total(acc)
            ratio = norm_next / norm_now
            norm_now = norm_next


def solve_kernel(
    anchor, wall, heads, flow, base, weight, nbr, vol, lift, jac, sel, spread, same,
    out, own_disp, disp, resid, search, image, diag, products, jumps, lifts, cand, pair, picked, flux,
):
    residual_parts(flow, heads, nbr, vol, lift, jac, sel, spread, same, products, jumps, lifts, cand, pair)
    solve_wall(wall, disp, resid, search, image, diag)
    sec, dom = lax.axis_index("sec"), lax.axis_index("dom")
    for c in range(3):
        for i in range(8):
            own_disp[c, pl.ds(i, 1), :] = disp[c * 256 + dom * 8 + i, pl.ds(sec, 1), :]
    lane = lax.broadcasted_iota(jnp.int32, (1, 128), 1)

    def pick(e, carry):
        a = anchor[e]
        line = a >> 7
        t, s, column = line & 255, line >> 8, a & 127
        hit = lane == column
        for c in range(3):
            value = disp[c * 256 + t, pl.ds(s, 1), :]
            picked[c, pl.ds(e, 1), :] = jnp.where(hit, value, 0.0)
        return carry

    lax.fori_loop(0, NE, pick, 0, unroll=8)
    ones = jnp.ones((8, 128), F32)
    geometry = []
    for k in range(4):
        row = base[pl.ds(k, 1), :]
        if k < 3:
            at = lax.dot_general(
                ones, picked[k], (((1,), (1,)), ((), ())), preferred_element_type=F32, precision=lax.Precision.HIGHEST
            )
            row = row * jnp.exp(weight[...] * at[:1])
        geometry.append(row)
    for face in range(6):
        rows = pl.ds(face * 128, 128)
        flux[rows, :] = (geometry[face // 2] * jumps[rows, :]).astype(BF16)
    total = dot(lifts[...], flux[...])
    for k in range(4):
        total = total + geometry[k] * products[k]
    out[...] = total.astype(BF16)


def on_device(flow_state, base_geometry, anchor_weight, wall_anchor, face_nbr, volume_ops, lift_ops, face_jac, wall_load, wall_stiff):
    wall, heads = exchange(wall_load, wall_stiff, flow_state)
    wall = wall.reshape(3, 2, 2048, 128)
    spread, same = expansion()
    vmem = pl.BlockSpec(memory_space=pltpu.VMEM)
    field = pltpu.VMEM((768, 8, 128), F32)
    return pl.pallas_call(
        solve_kernel,
        out_shape=(
            jax.ShapeDtypeStruct((NQ, NE), BF16),
            jax.ShapeDtypeStruct((3, 8, 128), F32),
        ),
        in_specs=[pl.BlockSpec(memory_space=pltpu.SMEM)] + [vmem] * 12,
        out_specs=(vmem, vmem),
        scratch_shapes=[
            field, field, field, field, field,
            pltpu.VMEM((4, NQ, NE), F32),
            pltpu.VMEM((768, NE), F32),
            pltpu.VMEM((NQ, 768), BF16),
            pltpu.VMEM((128, NE + HB), BF16),
            pltpu.VMEM((256, NE), BF16),
            pltpu.VMEM((3, NE, 128), F32),
            pltpu.VMEM((768, NE), BF16),
        ],
        compiler_params=pltpu.CompilerParams(vmem_limit_bytes=50 << 20),
        name="solve",
    )(
        wall_anchor, wall, heads, flow_state, base_geometry, anchor_weight.reshape(1, NE), face_nbr,
        volume_ops, lift_ops, face_jac,
        jnp.asarray(selection(), BF16), jnp.asarray(spread, BF16), jnp.asarray(same, F32),
    )


def solution(mesh):
    return jax.shard_map(
        on_device,
        mesh=mesh,
        in_specs=(
            P(None, ("sec", "dom")),
            P(None, ("sec", "dom")),
            P(("sec", "dom")),
            P(("sec", "dom")),
            P(None, ("sec", "dom")),
            P(),
            P(),
            P(),
            P(None, ("sec", "dom"), None),
            P(None, ("sec", "dom"), None),
        ),
        out_specs=(P(None, ("sec", "dom")), P(None, ("sec", "dom"), None)),
        check_vma=False,
    )
```

```python
import jax
import jax.numpy as jnp
import numpy as np
from jax import lax
from jax.experimental import pallas as pl
from jax.experimental.pallas import tpu as pltpu
from jax.sharding import PartitionSpec as P

MESH = pl.DeviceIdType.MESH
ITERS = 8
NQ = 270
NF = 90
NE = 1024
HB = 128
NY, NC, NX, NZ = 4, 2, 4, 8
SIZE = {"y": NY, "x": NX, "z": NZ}
ORDERS = (("z", "x", "y"), ("x", "y", "z"), ("z", "y", "x"))
SLOTS = 16
T = 256
UNROLL = 64
F32 = jnp.float32
BF16 = jnp.bfloat16


def selection():
    index = np.arange(NQ).reshape(5, 2, 3, 3, 3)
    rows = np.zeros((6, 128, NQ), np.float32)
    for face in range(6):
        picked = np.take(index, 0 if face % 2 == 0 else 2, axis=2 + face // 2).reshape(-1)
        rows[face, np.arange(NF), picked] = 1.0
    return rows


def expansion():
    spread = np.zeros((128, 5), np.float32)
    spread[np.arange(NF), np.arange(NF) // 18] = 1.0
    same = np.zeros((128, 128), np.float32)
    inside = np.arange(NF)
    same[:NF, :NF] = inside[:, None] % 18 == inside[None, :] % 18
    return spread, same


def coordinates():
    sec, dom = lax.axis_index("sec"), lax.axis_index("dom")
    return {"y": sec // NC, "core": sec % NC, "x": dom // NZ, "z": dom % NZ}


def device(place):
    return (place["y"] * NC + place["core"], place["x"] * NZ + place["z"])


def moved(place, axis, by):
    size = SIZE[axis]
    return dict(place, **{axis: (place[axis] + by + size) % size})


class Gather:
    def __init__(self, color, here, wall, send, recv, pass_send, pass_recv):
        self.color, self.here, self.wall = color, here, wall
        self.send, self.recv = send, recv
        self.pass_send, self.pass_recv = pass_send, pass_recv
        self.order = ORDERS[color]
        self.rounds = 2 + SIZE[self.order[2]] // 2
        self.made, self.passed, self.used = [], [], 0

    def block(self, stage, axis, at, half):
        index = {}
        for name in "yxz":
            if name in self.order[:stage]:
                index[name] = slice(None)
            elif name == axis:
                index[name] = at
            else:
                index[name] = self.here[name]
        which = slice(None) if half is None else half
        core = self.here["core"]
        if isinstance(index["y"], slice):
            line = pl.ds(pl.multiple_of(core * NY, NY), NY)
        else:
            line = core * NY + index["y"]
        return self.wall.at[self.color, which, index["x"], index["z"], :, line]

    def copy(self, stage, axis, at, half, target, sems, slot):
        source = self.block(stage, axis, at, half)
        copy = pltpu.make_async_remote_copy(
            src_ref=source,
            dst_ref=source,
            send_sem=sems[0].at[slot],
            recv_sem=sems[1].at[slot],
            device_id=device(target),
            device_id_type=MESH,
        )
        copy.start()
        return copy

    def launch(self, number):
        copies = []
        if number < 2:
            axis = self.order[number]
            for by in sorted(range(1, SIZE[axis]), key=lambda by: -min(by, SIZE[axis] - by)):
                slot = self.color * SLOTS + self.used
                self.used += 1
                copies.append(
                    self.copy(
                        number, axis, self.here[axis], None, moved(self.here, axis, by), (self.send, self.recv), slot
                    )
                )
        else:
            axis, step = self.order[2], number - 2
            size = SIZE[axis]
            for way, sign in enumerate((1, -1)):
                half = None if step < size // 2 - 1 else way
                at = (self.here[axis] - sign * step + size) % size
                slot = self.color * SLOTS + self.used
                self.used += 1
                copies.append(
                    self.copy(2, axis, at, half, moved(self.here, axis, sign), (self.send, self.recv), slot)
                )
            if step == 0:
                self.hand_over(self.here[axis])
        self.made.append(copies)

    def hand_over(self, at):
        slot = self.color * NZ + len(self.passed)
        partner = dict(self.here, core=1 - self.here["core"])
        sems = (self.pass_send, self.pass_recv)
        self.passed.append(self.copy(2, self.order[2], at, None, partner, sems, slot))

    def advance(self, number):
        if number > self.rounds:
            return
        if number > 0:
            for copy in self.made[number - 1]:
                copy.wait_recv()
        if number < self.rounds:
            self.launch(number)
        if number > 2:
            axis, step = self.order[2], number - 3
            size = SIZE[axis]
            self.hand_over((self.here[axis] - step - 1 + size) % size)
            if step < size // 2 - 1:
                self.hand_over((self.here[axis] + step + 1) % size)

    def finish(self):
        for copies in self.made:
            for copy in copies:
                copy.wait_send()
        for copy in self.passed:
            copy.wait()


def dot(a, b):
    return jnp.dot(a, b, preferred_element_type=F32)


def volume_part(direction, flow, vol, products):
    products[direction] = dot(vol[direction], flow[...])


def face_part(face, flow, heads, nbr, jac, sel, spread, same, jumps, cand):
    state = flow[...]
    row = lax.broadcasted_iota(jnp.int32, (256, 1), 0).astype(F32).astype(BF16)
    other = sel[face ^ 1]
    cand[:, pl.ds(0, NE)] = dot(other, state).astype(BF16)
    width = NE
    if face < 4:
        cand[:, pl.ds(NE, HB)] = dot(other, heads[face]).astype(BF16)
        width = NE + HB
    place = nbr[pl.ds(face, 1), :]
    theirs = jnp.zeros((128, NE), F32)
    for start in range(0, width, 256):
        size = min(256, width - start)
        key = jnp.where((place >= start) & (place < start + size), place - start, -1)
        key = key.astype(F32).astype(BF16)
        chosen = jnp.where(row[:size] == key, jnp.ones((), BF16), jnp.zeros((), BF16))
        theirs = theirs + dot(cand[:, pl.ds(start, size)], chosen)
    mine = dot(sel[face], state)
    mixes = []
    for side in range(2):
        wide = dot(spread[...], jac[face, side]).astype(BF16)
        wide = lax.dot_general(wide, spread[...], (((1,), (1,)), ((), ())), preferred_element_type=F32)
        mixes.append((wide * same[...]).astype(BF16))
    jumps[pl.ds(face * 128, 128), :] = dot(mixes[0], mine.astype(BF16)) + dot(mixes[1], theirs.astype(BF16))


def exchange_kernel(
    load, stiff, flow_in, nbr_in, vol_in, lift_in, jac_in, sel_in, spread_in, same_in,
    wall, products, jumps, lifts,
    heads, flow, nbr, vol, lift, jac, sel, spread, same, cand,
    send, recv, pass_send, pass_recv, head_send, head_recv, in_sem,
):
    here = coordinates()
    sec, dom = lax.axis_index("sec"), lax.axis_index("dom")
    n_sec, n_dom = NY * NC, NX * NZ
    sides = [
        (sec, (dom + 1) % n_dom),
        (sec, (dom + n_dom - 1) % n_dom),
        ((sec + 1) % n_sec, dom),
        ((sec + n_sec - 1) % n_sec, dom),
    ]
    peers = list(sides)
    for axis in "yxz":
        for by in range(1, SIZE[axis]):
            peers.append(device(moved(here, axis, by)))
    peers.append(device(dict(here, core=1 - here["core"])))
    barrier = pltpu.get_barrier_semaphore()
    for peer in peers:
        pl.semaphore_signal(barrier, inc=1, device_id=peer, device_id_type=MESH)
    line = here["core"] * NY + here["y"]
    pairs = [
        (load, wall.at[:, 0, here["x"], here["z"], :, line]),
        (stiff, wall.at[:, 1, here["x"], here["z"], :, line]),
        (flow_in, flow), (vol_in, vol), (nbr_in, nbr), (jac_in, jac),
        (sel_in, sel), (spread_in, spread), (same_in, same), (lift_in, lift),
    ]
    local = [pltpu.make_async_copy(a, b, in_sem.at[i]) for i, (a, b) in enumerate(pairs)]
    for copy in local:
        copy.start()
    lifts[...] = jnp.zeros_like(lifts)
    local[0].wait()
    local[1].wait()
    pl.semaphore_wait(barrier, len(peers))
    gathers = [Gather(color, here, wall, send, recv, pass_send, pass_recv) for color in range(3)]

    def advance(number):
        for gather in gathers:
            gather.advance(number)

    advance(0)
    head_copies = []
    for face, peer in enumerate(sides):
        copy = pltpu.make_async_remote_copy(
            src_ref=flow_in.at[:, pl.ds(0, HB)],
            dst_ref=heads.at[face],
            send_sem=head_send.at[face],
            recv_sem=head_recv.at[face],
            device_id=peer,
            device_id_type=MESH,
        )
        copy.start()
        head_copies.append(copy)
    for copy in local[2:]:
        copy.wait()

    def face(number):
        face_part(number, flow, heads, nbr, jac, sel, spread, same, jumps, cand)

    for direction in range(4):
        volume_part(direction, flow, vol, products)
    advance(1)
    for number in range(6):
        lifts[:, pl.ds(number * 128, NF)] = lift[number]
    face(4)
    face(5)
    advance(2)
    for copy in head_copies:
        copy.wait()
    face(0)
    advance(3)
    face(1)
    face(2)
    advance(4)
    face(3)
    advance(5)
    advance(6)
    for gather in gathers:
        gather.finish()


def stay(x):
    return pltpu.with_memory_space_constraint(x, pltpu.HBM)


def exchange(wall_load, wall_stiff, flow_state, face_nbr, volume_ops, lift_ops, face_jac):
    vmem = pl.BlockSpec(memory_space=pltpu.VMEM)
    far = pl.BlockSpec(memory_space=pltpu.HBM)
    spread, same = expansion()
    dma = pltpu.SemaphoreType.DMA
    return pl.pallas_call(
        exchange_kernel,
        out_shape=(
            jax.ShapeDtypeStruct((3, 2, NX, NZ, 8, NC * NY, 128), F32),
            jax.ShapeDtypeStruct((4, NQ, NE), F32),
            jax.ShapeDtypeStruct((768, NE), F32),
            jax.ShapeDtypeStruct((NQ, 768), BF16),
        ),
        in_specs=[far] * 10,
        out_specs=(vmem,) * 4,
        scratch_shapes=[
            pltpu.VMEM((4, NQ, HB), BF16),
            pltpu.VMEM((NQ, NE), BF16),
            pltpu.VMEM((6, NE), jnp.int32),
            pltpu.VMEM((4, NQ, NQ), BF16),
            pltpu.VMEM((6, NQ, NF), BF16),
            pltpu.VMEM((6, 2, 5, 5), BF16),
            pltpu.VMEM((6, 128, NQ), BF16),
            pltpu.VMEM((128, 5), BF16),
            pltpu.VMEM((128, 128), F32),
            pltpu.VMEM((128, NE + HB), BF16),
            dma((3 * SLOTS,)),
            dma((3 * SLOTS,)),
            dma((3 * NZ,)),
            dma((3 * NZ,)),
            dma((4,)),
            dma((4,)),
            dma((10,)),
        ],
        compiler_params=pltpu.CompilerParams(collective_id=0, has_side_effects=True, vmem_limit_bytes=32 << 20),
        name="exchange",
    )(
        *map(
            stay,
            (
                wall_load, wall_stiff, flow_state, face_nbr, volume_ops, lift_ops, face_jac,
                jnp.asarray(selection(), BF16), jnp.asarray(spread, BF16), jnp.asarray(same, F32),
            ),
        )
    )


def rows(i):
    return pl.ds(pl.multiple_of(i * 8, 8), 8)


def solve_wall(wall, disp, resid, searches, image, diag):
    lane = lax.broadcasted_iota(jnp.int32, (8, 128), 1)
    sub = lax.broadcasted_iota(jnp.int32, (8, 128), 0)
    zero = jnp.zeros((8, 128), F32)

    def total(acc):
        return jnp.sum(jnp.sum(acc, axis=0, keepdims=True), axis=1, keepdims=True)

    def previous(v):
        return jnp.where(sub >= 4, pltpu.roll(v, 4, 0), jnp.where(sub == 0, 0.0, pltpu.roll(v, 5, 0)))

    def following(v):
        return jnp.where(sub < 4, pltpu.roll(v, 4, 0), jnp.where(sub == 7, 0.0, pltpu.roll(v, 3, 0)))

    ratio = norm_now = None
    steps = []
    for iteration in range(ITERS):
        first, last = iteration == 0, iteration == ITERS - 1
        old, new = searches[(iteration + 1) % 2], searches[iteration % 2]
        if not first:
            ratio_b = jnp.broadcast_to(ratio, (8, 128))

        def direction(c, t):
            if first:
                return wall[c, 0, rows(t), :]
            return resid[rows(c * T + t), :] + ratio_b * old[rows(c * T + t), :]

        sums = (zero, zero)
        norms = (zero, zero)
        for c in range(3):
            top, bottom = direction(c, 0), direction(c, T - 1)

            def one(t, above, here, below, sums, norms):
                i = rows(c * T + t)
                left = jnp.where(lane == 0, 0.0, pltpu.roll(here, 1, 1))
                right = jnp.where(lane == 127, 0.0, pltpu.roll(here, 127, 1))
                if first:
                    middle = 4.0 + wall[c, 1, rows(t), :]
                    diag[i, :] = middle
                    norms = (norms[1], norms[0] + here * here)
                else:
                    middle = diag[i, :]
                value = middle * here - ((above + below) + (left + right))
                if not last:
                    image[i, :] = value
                new[i, :] = here
                return (sums[1], sums[0] + here * value), norms

            def block(b, carry, ends=False):
                above, here, sums, norms = carry
                for u in range(UNROLL):
                    t = b * UNROLL + u
                    if ends and u == UNROLL - 1:
                        below = following(top)
                    else:
                        below = direction(c, t + 1)
                    sums, norms = one(t, above, here, below, sums, norms)
                    above, here = here, below
                return above, here, sums, norms

            carry = (previous(bottom), top, sums, norms)
            carry = lax.fori_loop(0, T // UNROLL - 1, block, carry)
            _, _, sums, norms = block(T // UNROLL - 1, carry, ends=True)
        if first:
            norm_now = total(norms[0] + norms[1])
        step = jnp.broadcast_to(norm_now / total(sums[0] + sums[1]), (8, 128))
        steps.append(step)
        if first:
            source = [wall.at[c, 0] for c in range(3)]
        else:
            source = None

        def update(b, norms, c=None):
            for u in range(UNROLL // 2):
                t = b * (UNROLL // 2) + u
                i = rows(t if c is None else c * T + t)
                if iteration % 2 == 1:
                    gain = steps[iteration - 1] * old[i, :] + step * new[i, :]
                    disp[i, :] = gain if iteration == 1 else disp[i, :] + gain
                if not last:
                    held = source[c][rows(t), :] if first else resid[i, :]
                    held = held - step * image[i, :]
                    resid[i, :] = held
                    norms = (norms[1], norms[0] + held * held)
            return norms

        norms = (zero, zero)
        if first:
            for c in range(3):
                norms = lax.fori_loop(0, 2 * T // UNROLL, lambda b, n, c=c: update(b, n, c), norms)
        else:
            norms = lax.fori_loop(0, 6 * T // UNROLL, update, norms)
        if not last:
            norm_next = total(norms[0] + norms[1])
            ratio = norm_next / norm_now
            norm_now = norm_next


def solve_kernel(
    anchor_in, base_in, weight_in, wall, products, jumps, lifts,
    out, own_disp,
    disp, resid, search_a, search_b, image, diag, picked, flux, anchor, base, weight, in_sem,
):
    pairs = [(anchor_in, anchor), (base_in, base), (weight_in, weight)]
    local = [pltpu.make_async_copy(a, b, in_sem.at[i]) for i, (a, b) in enumerate(pairs)]
    for copy in local:
        copy.start()
    for copy in local:
        copy.wait()
    solve_wall(wall, disp, resid, (search_a, search_b), image, diag)
    sec, dom = lax.axis_index("sec"), lax.axis_index("dom")
    line = (sec % NC) * NY + sec // NC
    for c in range(3):
        for i in range(8):
            own_disp[c, pl.ds(i, 1), :] = disp[pl.ds((c * T + dom * 8 + i) * 8 + line, 1), :]
    lane = lax.broadcasted_iota(jnp.int32, (1, 128), 1)

    def pick(e, carry):
        a = anchor[e]
        s = a >> 15
        at = ((a >> 7) & (T - 1)) * 8 + (s & 1) * NY + (s >> 1)
        hit = lane == (a & 127)
        for c in range(3):
            picked[c, pl.ds(e, 1), :] = jnp.where(hit, disp[pl.ds(c * T * 8 + at, 1), :], 0.0)
        return carry

    lax.fori_loop(0, NE, pick, 0, unroll=16)
    ones = jnp.ones((8, 128), F32)
    geometry = []
    for k in range(4):
        row = base[pl.ds(k, 1), :]
        if k < 3:
            at = lax.dot_general(
                ones, picked[k], (((1,), (1,)), ((), ())), preferred_element_type=F32, precision=lax.Precision.HIGHEST
            )
            row = row * jnp.exp(weight[...] * at[:1])
        geometry.append(row)
    for face in range(6):
        at = pl.ds(face * 128, 128)
        flux[at, :] = (geometry[face // 2] * jumps[at, :]).astype(BF16)
    result = dot(lifts[...], flux[...])
    for k in range(4):
        result = result + geometry[k] * products[k]
    out[...] = result.astype(BF16)


def on_device(
    flow_state, base_geometry, anchor_weight, wall_anchor, face_nbr, volume_ops, lift_ops, face_jac, wall_load, wall_stiff
):
    wall, products, jumps, lifts = exchange(
        wall_load, wall_stiff, flow_state, face_nbr, volume_ops, lift_ops, face_jac
    )
    wall = wall.reshape(3, 2, T * 8, 128)
    vmem = pl.BlockSpec(memory_space=pltpu.VMEM)
    far = pl.BlockSpec(memory_space=pltpu.HBM)
    field = pltpu.VMEM((3 * T * 8, 128), F32)
    return pl.pallas_call(
        solve_kernel,
        out_shape=(
            jax.ShapeDtypeStruct((NQ, NE), BF16),
            jax.ShapeDtypeStruct((3, 8, 128), F32),
        ),
        in_specs=[far] * 3 + [vmem] * 4,
        out_specs=(vmem, vmem),
        scratch_shapes=[field] * 6
        + [
            pltpu.VMEM((3, NE, 128), F32),
            pltpu.VMEM((768, NE), BF16),
            pltpu.SMEM((NE,), jnp.int32),
            pltpu.VMEM((4, NE), F32),
            pltpu.VMEM((1, NE), F32),
            pltpu.SemaphoreType.DMA((3,)),
        ],
        compiler_params=pltpu.CompilerParams(vmem_limit_bytes=28 << 20),
        name="solve",
    )(
        *map(stay, (wall_anchor, base_geometry, anchor_weight.reshape(1, NE))), wall, products, jumps, lifts
    )


def solution(mesh):
    return jax.shard_map(
        on_device,
        mesh=mesh,
        in_specs=(
            P(None, ("sec", "dom")),
            P(None, ("sec", "dom")),
            P(("sec", "dom")),
            P(("sec", "dom")),
            P(None, ("sec", "dom")),
            P(),
            P(),
            P(),
            P(None, ("sec", "dom"), None),
            P(None, ("sec", "dom"), None),
        ),
        out_specs=(P(None, ("sec", "dom")), P(None, ("sec", "dom"), None)),
        check_vma=False,
    )
```

```python
import jax
import jax.numpy as jnp
import numpy as np
from jax import lax
from jax.experimental import pallas as pl
from jax.experimental.pallas import tpu as pltpu
from jax.sharding import PartitionSpec as P

MESH = pl.DeviceIdType.MESH
ITERS = 8
NQ = 270
NF = 90
NE = 1024
HB = 128
NY, NC, NX, NZ = 4, 2, 4, 8
SIZE = {"y": NY, "x": NX, "z": NZ}
ORDERS = (("z", "x", "y"), ("x", "y", "z"), ("z", "y", "x"))
SLOTS = 24
T = 256
UNROLL = 64
STIFF_LOW, STIFF_UNIT = 0.01, 0.29 / 65535.0
F32 = jnp.float32
BF16 = jnp.bfloat16


def selection():
    index = np.arange(NQ).reshape(5, 2, 3, 3, 3)
    rows = np.zeros((6, 128, NQ), np.float32)
    for face in range(6):
        picked = np.take(index, 0 if face % 2 == 0 else 2, axis=2 + face // 2).reshape(-1)
        rows[face, np.arange(NF), picked] = 1.0
    return rows


def expansion():
    spread = np.zeros((128, 5), np.float32)
    spread[np.arange(NF), np.arange(NF) // 18] = 1.0
    same = np.zeros((128, 128), np.float32)
    inside = np.arange(NF)
    same[:NF, :NF] = inside[:, None] % 18 == inside[None, :] % 18
    return spread, same


def coordinates():
    sec, dom = lax.axis_index("sec"), lax.axis_index("dom")
    return {"y": sec // NC, "core": sec % NC, "x": dom // NZ, "z": dom % NZ}


def device(place):
    return (place["y"] * NC + place["core"], place["x"] * NZ + place["z"])


def moved(place, axis, by):
    size = SIZE[axis]
    return dict(place, **{axis: (place[axis] + by + size) % size})


class Gather:
    def __init__(self, color, here, wall, send, recv, pass_send, pass_recv):
        self.color, self.here, self.wall = color, here, wall
        self.sems, self.pass_sems = (send, recv), (pass_send, pass_recv)
        self.order = ORDERS[color]
        self.size = SIZE[self.order[2]]
        self.reach = self.size // 2
        self.events = 4 + 2 * (self.reach - 1)
        self.lines, self.ring, self.passed = [[], []], {}, []
        self.used = 0

    def block(self, stage, axis, at, half):
        index = {}
        for name in "yxz":
            if name in self.order[:stage]:
                index[name] = slice(None)
            elif name == axis:
                index[name] = at
            else:
                index[name] = self.here[name]
        if half is not None:
            cut = "x" if axis != "x" else "z"
            index[cut] = pl.ds(half * (SIZE[cut] // 2), SIZE[cut] // 2)
        core = self.here["core"]
        if isinstance(index["y"], slice):
            line = pl.ds(pl.multiple_of(core * NY, NY), NY)
        else:
            line = core * NY + index["y"]
        return self.wall.at[self.color, index["x"], index["z"], :, line]

    def copy(self, stage, axis, at, half, target, sems, slot):
        source = self.block(stage, axis, at, half)
        copy = pltpu.make_async_remote_copy(
            src_ref=source,
            dst_ref=source,
            send_sem=sems[0].at[slot],
            recv_sem=sems[1].at[slot],
            device_id=device(target),
            device_id_type=MESH,
        )
        copy.start()
        return copy

    def slot(self):
        self.used += 1
        return self.color * SLOTS + self.used - 1

    def launch_line(self, number):
        axis = self.order[number]
        for by in sorted(range(1, SIZE[axis]), key=lambda by: -min(by, SIZE[axis] - by)):
            target = moved(self.here, axis, by)
            self.lines[number].append(
                self.copy(number, axis, self.here[axis], None, target, self.sems, self.slot())
            )

    def around(self, by):
        return (self.here[self.order[2]] + by + self.size) % self.size

    def launch_ring(self, step, half):
        for way, sign in enumerate((1, -1)):
            if step == self.reach - 1 and way != half:
                continue
            target = moved(self.here, self.order[2], sign)
            self.ring[step, half, way] = self.copy(
                2, self.order[2], self.around(-sign * step), half, target, self.sems, self.slot()
            )

    def hand_over(self, by, half):
        slot = self.color * 2 * NZ + len(self.passed)
        partner = dict(self.here, core=1 - self.here["core"])
        self.passed.append(self.copy(2, self.order[2], self.around(by), half, partner, self.pass_sems, slot))

    def advance(self, event):
        if event >= self.events:
            return
        if event < 2:
            if event == 1:
                for copy in self.lines[0]:
                    copy.wait_recv()
            self.launch_line(event)
        elif event == 2:
            for copy in self.lines[1]:
                copy.wait_recv()
            self.launch_ring(0, 0)
            self.launch_ring(0, 1)
            self.hand_over(0, 0)
            self.hand_over(0, 1)
        elif event < self.events - 1:
            step, half = (event - 3) // 2 + 1, (event - 3) % 2
            for way in range(2):
                self.ring[step - 1, half, way].wait_recv()
            self.launch_ring(step, half)
            self.hand_over(-step, half)
            self.hand_over(step, half)
        else:
            for half in range(2):
                self.ring[self.reach - 1, half, half].wait_recv()
                self.hand_over(self.reach, half)

    def finish(self):
        for copy in self.lines[0] + self.lines[1] + list(self.ring.values()):
            copy.wait_send()
        for copy in self.passed:
            copy.wait()


def dot(a, b):
    return jnp.dot(a, b, preferred_element_type=F32)


def pack_wall(load, stiff, out):
    largest = jnp.max(jnp.max(jnp.abs(load), axis=0, keepdims=True), axis=1, keepdims=True)
    power = jnp.ceil(jnp.log2(jnp.maximum(largest, 1e-30)) + 1e-4)
    power = jnp.broadcast_to(power, (1, 128)).astype(jnp.int32)
    unit = load_unit(power)
    high = jnp.clip(jnp.round(load / unit), -32767.0, 32767.0).astype(jnp.int32)
    low = jnp.clip(jnp.round((stiff - STIFF_LOW) / STIFF_UNIT), 0.0, 65535.0).astype(jnp.int32)
    word = (high << 16) | low
    for i in range(8):
        out[pl.ds(i, 1), :] = word[i : i + 1]
    out[pl.ds(8, 1), :] = power


def load_unit(power):
    return jnp.exp2(power.astype(F32)) * (1.0 / 32767.0)


def volume_part(direction, flow, vol, products):
    products[direction] = dot(vol[direction], flow[...])


def face_part(face, flow, heads, nbr, jac, sel, spread, same, jumps, cand):
    state = flow[...]
    row = lax.broadcasted_iota(jnp.int32, (256, 1), 0).astype(F32).astype(BF16)
    other = sel[face ^ 1]
    cand[:, pl.ds(0, NE)] = dot(other, state).astype(BF16)
    width = NE
    if face < 4:
        cand[:, pl.ds(NE, HB)] = dot(other, heads[face]).astype(BF16)
        width = NE + HB
    place = nbr[pl.ds(face, 1), :]
    theirs = jnp.zeros((128, NE), F32)
    for start in range(0, width, 256):
        size = min(256, width - start)
        key = jnp.where((place >= start) & (place < start + size), place - start, -1)
        key = key.astype(F32).astype(BF16)
        chosen = jnp.where(row[:size] == key, jnp.ones((), BF16), jnp.zeros((), BF16))
        theirs = theirs + dot(cand[:, pl.ds(start, size)], chosen)
    mine = dot(sel[face], state)
    mixes = []
    for side in range(2):
        wide = dot(spread[...], jac[face, side]).astype(BF16)
        wide = lax.dot_general(wide, spread[...], (((1,), (1,)), ((), ())), preferred_element_type=F32)
        mixes.append((wide * same[...]).astype(BF16))
    jumps[pl.ds(face * 128, 128), :] = dot(mixes[0], mine.astype(BF16)) + dot(mixes[1], theirs.astype(BF16))


def exchange_kernel(
    load, stiff, flow_in, nbr_in, vol, lift_in, jac, sel_in, spread_in, same_in,
    wall, products, jumps, lifts,
    heads, flow, nbr, lift, sel, spread, same, cand, own_load, own_stiff,
    send, recv, pass_send, pass_recv, head_send, head_recv, in_sem,
):
    here = coordinates()
    sec, dom = lax.axis_index("sec"), lax.axis_index("dom")
    n_sec, n_dom = NY * NC, NX * NZ
    sides = [
        (sec, (dom + 1) % n_dom),
        (sec, (dom + n_dom - 1) % n_dom),
        ((sec + 1) % n_sec, dom),
        ((sec + n_sec - 1) % n_sec, dom),
    ]
    peers = list(sides)
    for axis in "yxz":
        for by in range(1, SIZE[axis]):
            peers.append(device(moved(here, axis, by)))
    peers.append(device(dict(here, core=1 - here["core"])))
    barrier = pltpu.get_barrier_semaphore()
    for peer in peers:
        pl.semaphore_signal(barrier, inc=1, device_id=peer, device_id_type=MESH)
    pairs = [
        (load, own_load), (stiff, own_stiff), (flow_in, flow), (nbr_in, nbr),
        (sel_in, sel), (spread_in, spread), (same_in, same), (lift_in, lift),
    ]
    local = [pltpu.make_async_copy(a, b, in_sem.at[i]) for i, (a, b) in enumerate(pairs)]
    for copy in local:
        copy.start()
    local[0].wait()
    local[1].wait()
    line = here["core"] * NY + here["y"]
    for c in range(3):
        pack_wall(own_load[c], own_stiff[c], wall.at[c, here["x"], here["z"], :, line])
    lifts[...] = jnp.zeros_like(lifts)
    pl.semaphore_wait(barrier, len(peers))
    gathers = [Gather(color, here, wall, send, recv, pass_send, pass_recv) for color in range(3)]

    def advance(*events):
        for event in events:
            for gather in gathers:
                gather.advance(event)

    advance(0)
    for copy in local[2:]:
        copy.wait()
    for direction in range(4):
        volume_part(direction, flow, vol, products)
    advance(1)
    head_copies = []
    for face, peer in enumerate(sides):
        copy = pltpu.make_async_remote_copy(
            src_ref=flow_in.at[:, pl.ds(0, HB)],
            dst_ref=heads.at[face],
            send_sem=head_send.at[face],
            recv_sem=head_recv.at[face],
            device_id=peer,
            device_id_type=MESH,
        )
        copy.start()
        head_copies.append(copy)

    def face(number):
        face_part(number, flow, heads, nbr, jac, sel, spread, same, jumps, cand)

    for number in range(6):
        lifts[:, pl.ds(number * 128, NF)] = lift[number]
    face(4)
    face(5)
    advance(2)
    for copy in head_copies:
        copy.wait()
    face(0)
    advance(3)
    face(1)
    advance(4)
    face(2)
    advance(5, 6)
    face(3)
    advance(7, 8, 9)
    for gather in gathers:
        gather.finish()


def stay(x):
    return pltpu.with_memory_space_constraint(x, pltpu.HBM)


def exchange(wall_load, wall_stiff, flow_state, face_nbr, volume_ops, lift_ops, face_jac):
    vmem = pl.BlockSpec(memory_space=pltpu.VMEM)
    far = pl.BlockSpec(memory_space=pltpu.HBM)
    spread, same = expansion()
    dma = pltpu.SemaphoreType.DMA
    return pl.pallas_call(
        exchange_kernel,
        out_shape=(
            jax.ShapeDtypeStruct((3, NX, NZ, 9, NC * NY, 128), jnp.int32),
            jax.ShapeDtypeStruct((4, NQ, NE), F32),
            jax.ShapeDtypeStruct((768, NE), F32),
            jax.ShapeDtypeStruct((NQ, 768), BF16),
        ),
        in_specs=[far] * 4 + [vmem, far, vmem] + [far] * 3,
        out_specs=(vmem,) * 4,
        scratch_shapes=[
            pltpu.VMEM((4, NQ, HB), BF16),
            pltpu.VMEM((NQ, NE), BF16),
            pltpu.VMEM((6, NE), jnp.int32),
            pltpu.VMEM((6, NQ, NF), BF16),
            pltpu.VMEM((6, 128, NQ), BF16),
            pltpu.VMEM((128, 5), BF16),
            pltpu.VMEM((128, 128), F32),
            pltpu.VMEM((128, NE + HB), BF16),
            pltpu.VMEM((3, 8, 128), F32),
            pltpu.VMEM((3, 8, 128), F32),
            dma((3 * SLOTS,)),
            dma((3 * SLOTS,)),
            dma((3 * 2 * NZ,)),
            dma((3 * 2 * NZ,)),
            dma((4,)),
            dma((4,)),
            dma((8,)),
        ],
        compiler_params=pltpu.CompilerParams(collective_id=0, has_side_effects=True, vmem_limit_bytes=32 << 20),
        name="exchange",
    )(
        *map(stay, (wall_load, wall_stiff, flow_state, face_nbr)),
        volume_ops,
        stay(lift_ops),
        face_jac,
        *map(stay, (jnp.asarray(selection(), BF16), jnp.asarray(spread, BF16), jnp.asarray(same, F32))),
    )


def rows(i):
    return pl.ds(pl.multiple_of(i * 8, 8), 8)


def solve_wall(wall, disp, resid, searches, image, diag):
    lane = lax.broadcasted_iota(jnp.int32, (8, 128), 1)
    sub = lax.broadcasted_iota(jnp.int32, (8, 128), 0)
    zero = jnp.zeros((8, 128), F32)

    def total(acc):
        return jnp.sum(jnp.sum(acc, axis=0, keepdims=True), axis=1, keepdims=True)

    def previous(v):
        return jnp.where(sub >= 4, pltpu.roll(v, 4, 0), jnp.where(sub == 0, 0.0, pltpu.roll(v, 5, 0)))

    def following(v):
        return jnp.where(sub < 4, pltpu.roll(v, 4, 0), jnp.where(sub == 7, 0.0, pltpu.roll(v, 3, 0)))

    ratio = norm_now = None
    steps = []
    for iteration in range(ITERS):
        first, last = iteration == 0, iteration == ITERS - 1
        old, new = searches[(iteration + 1) % 2], searches[iteration % 2]
        if not first:
            ratio_b = jnp.broadcast_to(ratio, (8, 128))

        def direction(c, b, u):
            if not first:
                i = rows(c * T + b * UNROLL + u)
                return resid[i, :] + ratio_b * old[i, :]
            group = (c * T + b * UNROLL) // 8 + u // 8
            if (c, u // 8) not in units:
                units[c, u // 8] = load_unit(wall[rows(group * 9 + 8), :])
            return (wall[rows(group * 9 + u % 8), :] >> 16).astype(F32) * units[c, u // 8]

        def stiffness(c, b, u):
            group = (c * T + b * UNROLL) // 8 + u // 8
            code = wall[rows(group * 9 + u % 8), :] & 65535
            return (4.0 + STIFF_LOW) + code.astype(F32) * STIFF_UNIT

        sums = (zero, zero)
        norms = (zero, zero)
        for c in range(3):
            units = {}
            top = direction(c, 0, 0)
            units = {}
            bottom = direction(c, T // UNROLL - 1, UNROLL - 1)

            def one(b, u, above, here, below, sums, norms):
                i = rows(c * T + b * UNROLL + u)
                left = jnp.where(lane == 0, 0.0, pltpu.roll(here, 1, 1))
                right = jnp.where(lane == 127, 0.0, pltpu.roll(here, 127, 1))
                if first:
                    middle = stiffness(c, b, u)
                    diag[i, :] = middle
                    norms = (norms[1], norms[0] + here * here)
                else:
                    middle = diag[i, :]
                value = middle * here - ((above + below) + (left + right))
                if not last:
                    image[i, :] = value
                new[i, :] = here
                return (sums[1], sums[0] + here * value), norms

            def block(b, carry, ends=False):
                above, here, sums, norms = carry
                units.clear()
                for u in range(UNROLL):
                    if ends and u == UNROLL - 1:
                        below = following(top)
                    else:
                        below = direction(c, b, u + 1)
                    sums, norms = one(b, u, above, here, below, sums, norms)
                    above, here = here, below
                return above, here, sums, norms

            carry = (previous(bottom), top, sums, norms)
            carry = lax.fori_loop(0, T // UNROLL - 1, block, carry)
            _, _, sums, norms = block(T // UNROLL - 1, carry, ends=True)
        if first:
            norm_now = total(norms[0] + norms[1])
        step = jnp.broadcast_to(norm_now / total(sums[0] + sums[1]), (8, 128))
        steps.append(step)
        def update(b, norms):
            for u in range(UNROLL // 2):
                i = rows(b * (UNROLL // 2) + u)
                if iteration % 2 == 1:
                    gain = steps[iteration - 1] * old[i, :] + step * new[i, :]
                    disp[i, :] = gain if iteration == 1 else disp[i, :] + gain
                if not last:
                    held = (new if first else resid)[i, :] - step * image[i, :]
                    resid[i, :] = held
                    norms = (norms[1], norms[0] + held * held)
            return norms

        norms = (zero, zero)
        norms = lax.fori_loop(0, 6 * T // UNROLL, update, norms)
        if not last:
            norm_next = total(norms[0] + norms[1])
            ratio = norm_next / norm_now
            norm_now = norm_next


def solve_kernel(
    anchor_in, base_in, weight_in, wall, products, jumps, lifts,
    out, own_disp,
    disp, resid, search_a, search_b, image, diag, picked, flux, anchor, base, weight, in_sem,
):
    pairs = [(anchor_in, anchor), (base_in, base), (weight_in, weight)]
    local = [pltpu.make_async_copy(a, b, in_sem.at[i]) for i, (a, b) in enumerate(pairs)]
    for copy in local:
        copy.start()
    for copy in local:
        copy.wait()
    solve_wall(wall, disp, resid, (search_a, search_b), image, diag)
    sec, dom = lax.axis_index("sec"), lax.axis_index("dom")
    line = (sec % NC) * NY + sec // NC
    for c in range(3):
        for i in range(8):
            own_disp[c, pl.ds(i, 1), :] = disp[pl.ds((c * T + dom * 8 + i) * 8 + line, 1), :]
    lane = lax.broadcasted_iota(jnp.int32, (1, 128), 1)

    def pick(e, carry):
        a = anchor[e]
        s = a >> 15
        at = ((a >> 7) & (T - 1)) * 8 + (s & 1) * NY + (s >> 1)
        hit = lane == (a & 127)
        for c in range(3):
            picked[c, pl.ds(e, 1), :] = jnp.where(hit, disp[pl.ds(c * T * 8 + at, 1), :], 0.0)
        return carry

    lax.fori_loop(0, NE, pick, 0, unroll=16)
    ones = jnp.ones((8, 128), F32)
    geometry = []
    for k in range(4):
        row = base[pl.ds(k, 1), :]
        if k < 3:
            at = lax.dot_general(
                ones, picked[k], (((1,), (1,)), ((), ())), preferred_element_type=F32, precision=lax.Precision.HIGHEST
            )
            row = row * jnp.exp(weight[...] * at[:1])
        geometry.append(row)
    for face in range(6):
        at = pl.ds(face * 128, 128)
        flux[at, :] = (geometry[face // 2] * jumps[at, :]).astype(BF16)
    result = dot(lifts[...], flux[...])
    for k in range(4):
        result = result + geometry[k] * products[k]
    out[...] = result.astype(BF16)


def on_device(
    flow_state, base_geometry, anchor_weight, wall_anchor, face_nbr, volume_ops, lift_ops, face_jac, wall_load, wall_stiff
):
    wall, products, jumps, lifts = exchange(
        wall_load, wall_stiff, flow_state, face_nbr, volume_ops, lift_ops, face_jac
    )
    wall = wall.reshape(3 * T * 9, 128)
    vmem = pl.BlockSpec(memory_space=pltpu.VMEM)
    far = pl.BlockSpec(memory_space=pltpu.HBM)
    field = pltpu.VMEM((3 * T * 8, 128), F32)
    return pl.pallas_call(
        solve_kernel,
        out_shape=(
            jax.ShapeDtypeStruct((NQ, NE), BF16),
            jax.ShapeDtypeStruct((3, 8, 128), F32),
        ),
        in_specs=[far] * 3 + [vmem] * 4,
        out_specs=(vmem, vmem),
        scratch_shapes=[field] * 6
        + [
            pltpu.VMEM((3, NE, 128), F32),
            pltpu.VMEM((768, NE), BF16),
            pltpu.SMEM((NE,), jnp.int32),
            pltpu.VMEM((4, NE), F32),
            pltpu.VMEM((1, NE), F32),
            pltpu.SemaphoreType.DMA((3,)),
        ],
        compiler_params=pltpu.CompilerParams(vmem_limit_bytes=28 << 20),
        name="solve",
    )(
        *map(stay, (wall_anchor, base_geometry, anchor_weight.reshape(1, NE))), wall, products, jumps, lifts
    )


def solution(mesh):
    return jax.shard_map(
        on_device,
        mesh=mesh,
        in_specs=(
            P(None, ("sec", "dom")),
            P(None, ("sec", "dom")),
            P(("sec", "dom")),
            P(("sec", "dom")),
            P(None, ("sec", "dom")),
            P(),
            P(),
            P(),
            P(None, ("sec", "dom"), None),
            P(None, ("sec", "dom"), None),
        ),
        out_specs=(P(None, ("sec", "dom")), P(None, ("sec", "dom"), None)),
        check_vma=False,
    )
```

```python
import jax
import jax.numpy as jnp
import numpy as np
from jax import lax
from jax.experimental import pallas as pl
from jax.experimental.pallas import tpu as pltpu
from jax.sharding import PartitionSpec as P

MESH = pl.DeviceIdType.MESH
ITERS = 8
NQ = 270
NF = 90
NE = 1024
HB = 128
NY, NC, NX, NZ = 4, 2, 4, 8
SIZE = {"y": NY, "x": NX, "z": NZ}
ORDERS = (("z", "x", "y"), ("x", "y", "z"), ("z", "y", "x"))
SLOTS = 24
T = 256
UNROLL = 256
BUNROLL = 64
STIFF_LOW, STIFF_UNIT = 0.01, 0.29 / 65535.0
F32 = jnp.float32
BF16 = jnp.bfloat16


def selection():
    index = np.arange(NQ).reshape(5, 2, 3, 3, 3)
    rows = np.zeros((6, 128, NQ), np.float32)
    for face in range(6):
        picked = np.take(index, 0 if face % 2 == 0 else 2, axis=2 + face // 2).reshape(-1)
        rows[face, np.arange(NF), picked] = 1.0
    return rows


def expansion():
    spread = np.zeros((128, 5), np.float32)
    spread[np.arange(NF), np.arange(NF) // 18] = 1.0
    same = np.zeros((128, 128), np.float32)
    inside = np.arange(NF)
    same[:NF, :NF] = inside[:, None] % 18 == inside[None, :] % 18
    return spread, same


def coordinates():
    sec, dom = lax.axis_index("sec"), lax.axis_index("dom")
    return {"y": sec // NC, "core": sec % NC, "x": dom // NZ, "z": dom % NZ}


def device(place):
    return (place["y"] * NC + place["core"], place["x"] * NZ + place["z"])


def moved(place, axis, by):
    size = SIZE[axis]
    return dict(place, **{axis: (place[axis] + by + size) % size})


class Gather:
    def __init__(self, color, here, wall, send, recv, pass_send, pass_recv):
        self.color, self.here, self.wall = color, here, wall
        self.sems, self.pass_sems = (send, recv), (pass_send, pass_recv)
        self.order = ORDERS[color]
        self.size = SIZE[self.order[2]]
        self.reach = self.size // 2
        self.events = 4 + 2 * (self.reach - 1)
        self.lines, self.ring, self.passed = [[], []], {}, []
        self.used = 0

    def block(self, stage, axis, at, half):
        index = {}
        for name in "yxz":
            if name in self.order[:stage]:
                index[name] = slice(None)
            elif name == axis:
                index[name] = at
            else:
                index[name] = self.here[name]
        if half is not None:
            cut = "x" if axis != "x" else "z"
            index[cut] = pl.ds(half * (SIZE[cut] // 2), SIZE[cut] // 2)
        core = self.here["core"]
        if isinstance(index["y"], slice):
            line = pl.ds(pl.multiple_of(core * NY, NY), NY)
        else:
            line = core * NY + index["y"]
        return self.wall.at[self.color, index["x"], index["z"], :, line]

    def copy(self, stage, axis, at, half, target, sems, slot):
        source = self.block(stage, axis, at, half)
        copy = pltpu.make_async_remote_copy(
            src_ref=source,
            dst_ref=source,
            send_sem=sems[0].at[slot],
            recv_sem=sems[1].at[slot],
            device_id=device(target),
            device_id_type=MESH,
        )
        copy.start()
        return copy

    def slot(self):
        self.used += 1
        return self.color * SLOTS + self.used - 1

    def launch_line(self, number):
        axis = self.order[number]
        for by in sorted(range(1, SIZE[axis]), key=lambda by: -min(by, SIZE[axis] - by)):
            target = moved(self.here, axis, by)
            self.lines[number].append(
                self.copy(number, axis, self.here[axis], None, target, self.sems, self.slot())
            )

    def around(self, by):
        return (self.here[self.order[2]] + by + self.size) % self.size

    def launch_ring(self, step, half):
        for way, sign in enumerate((1, -1)):
            if step == self.reach - 1 and way != half:
                continue
            target = moved(self.here, self.order[2], sign)
            self.ring[step, half, way] = self.copy(
                2, self.order[2], self.around(-sign * step), half, target, self.sems, self.slot()
            )

    def hand_over(self, by, half):
        slot = self.color * 2 * NZ + len(self.passed)
        partner = dict(self.here, core=1 - self.here["core"])
        self.passed.append(self.copy(2, self.order[2], self.around(by), half, partner, self.pass_sems, slot))

    def advance(self, event):
        if event >= self.events:
            return
        if event < 2:
            if event == 1:
                for copy in self.lines[0]:
                    copy.wait_recv()
            self.launch_line(event)
        elif event == 2:
            for copy in self.lines[1]:
                copy.wait_recv()
            self.launch_ring(0, 0)
            self.launch_ring(0, 1)
            self.hand_over(0, 0)
            self.hand_over(0, 1)
        elif event < self.events - 1:
            step, half = (event - 3) // 2 + 1, (event - 3) % 2
            for way in range(2):
                self.ring[step - 1, half, way].wait_recv()
            self.launch_ring(step, half)
            self.hand_over(-step, half)
            self.hand_over(step, half)
        else:
            for half in range(2):
                self.ring[self.reach - 1, half, half].wait_recv()
                self.hand_over(self.reach, half)

    def finish(self):
        for copy in self.lines[0] + self.lines[1] + list(self.ring.values()):
            copy.wait_send()
        for copy in self.passed:
            copy.wait()


def dot(a, b):
    return jnp.dot(a, b, preferred_element_type=F32)


def pack_wall(load, stiff, out):
    largest = jnp.max(jnp.max(jnp.abs(load), axis=0, keepdims=True), axis=1, keepdims=True)
    power = jnp.ceil(jnp.log2(jnp.maximum(largest, 1e-30)) + 1e-4)
    power = jnp.broadcast_to(power, (1, 128)).astype(jnp.int32)
    unit = load_unit(power)
    high = jnp.clip(jnp.round(load / unit), -32767.0, 32767.0).astype(jnp.int32)
    low = jnp.clip(jnp.round((stiff - STIFF_LOW) / STIFF_UNIT), 0.0, 65535.0).astype(jnp.int32)
    word = (high << 16) | low
    for i in range(8):
        out[pl.ds(i, 1), :] = word[i : i + 1]
    out[pl.ds(8, 1), :] = power


def load_unit(power):
    return jnp.exp2(power.astype(F32)) * (1.0 / 32767.0)


def find_anchors(anchor, lines, columns):
    place = anchor[...]
    section = place >> 15
    lines[...] = ((place >> 7) & (T - 1)) * 8 + (section & 1) * NY + (section >> 1)
    column = lax.broadcasted_iota(jnp.int32, (128, 1), 0)
    columns[...] = jnp.where(column == (place & 127), 1.0, 0.0)


def volume_part(direction, flow, vol, products):
    products[direction] = dot(vol[direction], flow[...])


def face_part(face, flow, heads, nbr, jac, sel, spread, same, jumps, cand):
    state = flow[...]
    row = lax.broadcasted_iota(jnp.int32, (256, 1), 0).astype(F32).astype(BF16)
    other = sel[face ^ 1]
    cand[:, pl.ds(0, NE)] = dot(other, state).astype(BF16)
    width = NE
    if face < 4:
        cand[:, pl.ds(NE, HB)] = dot(other, heads[face]).astype(BF16)
        width = NE + HB
    place = nbr[pl.ds(face, 1), :]
    theirs = jnp.zeros((128, NE), F32)
    for start in range(0, width, 256):
        size = min(256, width - start)
        key = jnp.where((place >= start) & (place < start + size), place - start, -1)
        key = key.astype(F32).astype(BF16)
        chosen = jnp.where(row[:size] == key, jnp.ones((), BF16), jnp.zeros((), BF16))
        theirs = theirs + dot(cand[:, pl.ds(start, size)], chosen)
    mine = dot(sel[face], state)
    mixes = []
    for side in range(2):
        wide = dot(spread[...], jac[face, side]).astype(BF16)
        wide = lax.dot_general(wide, spread[...], (((1,), (1,)), ((), ())), preferred_element_type=F32)
        mixes.append((wide * same[...]).astype(BF16))
    jumps[pl.ds(face * 128, 128), :] = dot(mixes[0], mine.astype(BF16)) + dot(mixes[1], theirs.astype(BF16))


def exchange_kernel(
    load, stiff, flow_in, nbr_in, anchor_in, vol, lift_in, jac, sel_in, spread_in, same_in,
    wall, products, jumps, lifts, lines, columns,
    heads, flow, nbr, anchor, lift, sel, spread, same, cand, own_load, own_stiff,
    send, recv, pass_send, pass_recv, head_send, head_recv, in_sem,
):
    here = coordinates()
    sec, dom = lax.axis_index("sec"), lax.axis_index("dom")
    n_sec, n_dom = NY * NC, NX * NZ
    sides = [
        (sec, (dom + 1) % n_dom),
        (sec, (dom + n_dom - 1) % n_dom),
        ((sec + 1) % n_sec, dom),
        ((sec + n_sec - 1) % n_sec, dom),
    ]
    peers = list(sides)
    for axis in "yxz":
        for by in range(1, SIZE[axis]):
            peers.append(device(moved(here, axis, by)))
    peers.append(device(dict(here, core=1 - here["core"])))
    barrier = pltpu.get_barrier_semaphore()
    for peer in peers:
        pl.semaphore_signal(barrier, inc=1, device_id=peer, device_id_type=MESH)
    pairs = [
        (load, own_load), (stiff, own_stiff), (flow_in, flow), (nbr_in, nbr), (anchor_in, anchor),
        (sel_in, sel), (spread_in, spread), (same_in, same), (lift_in, lift),
    ]
    local = [pltpu.make_async_copy(a, b, in_sem.at[i]) for i, (a, b) in enumerate(pairs)]
    for copy in local:
        copy.start()
    local[0].wait()
    local[1].wait()
    line = here["core"] * NY + here["y"]
    for c in range(3):
        pack_wall(own_load[c], own_stiff[c], wall.at[c, here["x"], here["z"], :, line])
    lifts[...] = jnp.zeros_like(lifts)
    pl.semaphore_wait(barrier, len(peers))
    gathers = [Gather(color, here, wall, send, recv, pass_send, pass_recv) for color in range(3)]

    def advance(*pairs):
        for color, event in pairs:
            gathers[color].advance(event)

    def face(number):
        face_part(number, flow, heads, nbr, jac, sel, spread, same, jumps, cand)

    advance((1, 0), (0, 0), (2, 0))
    head_copies = []
    for number, peer in enumerate(sides):
        copy = pltpu.make_async_remote_copy(
            src_ref=flow_in.at[:, pl.ds(0, HB)],
            dst_ref=heads.at[number],
            send_sem=head_send.at[number],
            recv_sem=head_recv.at[number],
            device_id=peer,
            device_id_type=MESH,
        )
        copy.start()
        head_copies.append(copy)
    for copy in local[2:]:
        copy.wait()
    for direction in range(4):
        volume_part(direction, flow, vol, products)
    advance((1, 1), (0, 1), (2, 1))
    find_anchors(anchor, lines, columns)
    for number in range(6):
        lifts[:, pl.ds(number * 128, NF)] = lift[number]
    face(4)
    face(5)
    advance((1, 2), (0, 2), (2, 2))
    for copy in head_copies:
        copy.wait()
    face(0)
    advance((1, 3), (1, 4), (0, 3), (2, 3))
    face(1)
    advance((1, 5), (1, 6), (0, 4), (2, 4))
    face(2)
    advance((1, 7), (1, 8), (0, 5), (2, 5))
    face(3)
    advance((1, 9),)
    for gather in gathers:
        gather.finish()


def stay(x):
    return pltpu.with_memory_space_constraint(x, pltpu.HBM)


def exchange(wall_load, wall_stiff, flow_state, face_nbr, wall_anchor, volume_ops, lift_ops, face_jac):
    vmem = pl.BlockSpec(memory_space=pltpu.VMEM)
    far = pl.BlockSpec(memory_space=pltpu.HBM)
    spread, same = expansion()
    dma = pltpu.SemaphoreType.DMA
    return pl.pallas_call(
        exchange_kernel,
        out_shape=(
            jax.ShapeDtypeStruct((3, NX, NZ, 9, NC * NY, 128), jnp.int32),
            jax.ShapeDtypeStruct((4, NQ, NE), F32),
            jax.ShapeDtypeStruct((768, NE), F32),
            jax.ShapeDtypeStruct((NQ, 768), BF16),
            jax.ShapeDtypeStruct((1, NE), jnp.int32),
            jax.ShapeDtypeStruct((128, NE), F32),
        ),
        in_specs=[far] * 5 + [vmem, far, vmem] + [far] * 3,
        out_specs=(vmem,) * 6,
        scratch_shapes=[
            pltpu.VMEM((4, NQ, HB), BF16),
            pltpu.VMEM((NQ, NE), BF16),
            pltpu.VMEM((6, NE), jnp.int32),
            pltpu.VMEM((1, NE), jnp.int32),
            pltpu.VMEM((6, NQ, NF), BF16),
            pltpu.VMEM((6, 128, NQ), BF16),
            pltpu.VMEM((128, 5), BF16),
            pltpu.VMEM((128, 128), F32),
            pltpu.VMEM((128, NE + HB), BF16),
            pltpu.VMEM((3, 8, 128), F32),
            pltpu.VMEM((3, 8, 128), F32),
            dma((3 * SLOTS,)),
            dma((3 * SLOTS,)),
            dma((3 * 2 * NZ,)),
            dma((3 * 2 * NZ,)),
            dma((4,)),
            dma((4,)),
            dma((9,)),
        ],
        compiler_params=pltpu.CompilerParams(collective_id=0, has_side_effects=True, vmem_limit_bytes=32 << 20),
        name="exchange",
    )(
        *map(stay, (wall_load, wall_stiff, flow_state, face_nbr, wall_anchor.reshape(1, NE))),
        volume_ops,
        stay(lift_ops),
        face_jac,
        *map(stay, (jnp.asarray(selection(), BF16), jnp.asarray(spread, BF16), jnp.asarray(same, F32))),
    )


def rows(i):
    return pl.ds(pl.multiple_of(i * 8, 8), 8)


def solve_wall(wall, disp, resid, searches, image, diag):
    lane = lax.broadcasted_iota(jnp.int32, (8, 128), 1)
    sub = lax.broadcasted_iota(jnp.int32, (8, 128), 0)
    zero = jnp.zeros((8, 128), F32)

    def total(acc):
        return jnp.sum(jnp.sum(acc, axis=0, keepdims=True), axis=1, keepdims=True)

    def wide(value):
        return jnp.broadcast_to(value, (8, 128))

    def previous(v):
        return jnp.where(sub >= 4, pltpu.roll(v, 4, 0), jnp.where(sub == 0, 0.0, pltpu.roll(v, 5, 0)))

    def following(v):
        return jnp.where(sub < 4, pltpu.roll(v, 4, 0), jnp.where(sub == 7, 0.0, pltpu.roll(v, 3, 0)))

    def apply(old, new, ratio, first=False, last=False):
        units = {}

        def packed(c, b, u):
            group = (c * T + b * UNROLL) // 8 + u // 8
            return group, wall[rows(group * 9 + u % 8), :]

        def direction(c, b, u):
            if not first:
                i = rows(c * T + b * UNROLL + u)
                return resid[i, :] + ratio * old[i, :]
            group, word = packed(c, b, u)
            if u // 8 not in units:
                units[u // 8] = load_unit(wall[rows(group * 9 + 8), :])
            return (word >> 16).astype(F32) * units[u // 8]

        sums = norms = (zero, zero)
        for c in range(3):
            units.clear()
            top = direction(c, 0, 0)
            units.clear()
            bottom = direction(c, T // UNROLL - 1, UNROLL - 1)

            def block(b, carry, ends=False):
                above, here, sums, norms = carry
                units.clear()
                for u in range(UNROLL):
                    i = rows(c * T + b * UNROLL + u)
                    below = following(top) if ends and u == UNROLL - 1 else direction(c, b, u + 1)
                    left = jnp.where(lane == 0, 0.0, pltpu.roll(here, 1, 1))
                    right = jnp.where(lane == 127, 0.0, pltpu.roll(here, 127, 1))
                    if first:
                        code = packed(c, b, u)[1] & 65535
                        middle = (4.0 + STIFF_LOW) + code.astype(F32) * STIFF_UNIT
                        diag[i, :] = middle
                        norms = (norms[1], norms[0] + here * here)
                    else:
                        middle = diag[i, :]
                    value = middle * here - ((above + below) + (left + right))
                    if not last:
                        image[i, :] = value
                    new[i, :] = here
                    sums = (sums[1], sums[0] + here * value)
                    above, here = here, below
                return above, here, sums, norms

            carry = (previous(bottom), top, sums, norms)
            if T > UNROLL:
                carry = lax.fori_loop(0, T // UNROLL - 1, block, carry)
            _, _, sums, norms = block(T // UNROLL - 1, carry, ends=True)
        return total(sums[0] + sums[1]), total(norms[0] + norms[1]) if first else None

    def update(step, source, moves, add=True, norm=True):
        def block(b, norms):
            for u in range(BUNROLL):
                i = rows(b * BUNROLL + u)
                if moves:
                    gain = moves[0][0] * moves[0][1][i, :]
                    for size, field in moves[1:]:
                        gain = gain + size * field[i, :]
                    disp[i, :] = disp[i, :] + gain if add else gain
                if norm:
                    held = source[i, :] - step * image[i, :]
                    resid[i, :] = held
                    norms = (norms[1], norms[0] + held * held)
            return norms

        norms = lax.fori_loop(0, 3 * T // BUNROLL, block, (zero, zero))
        return total(norms[0] + norms[1]) if norm else None

    even, odd = searches
    product, norm = apply(None, even, None, first=True)
    step = wide(norm / product)
    norm_next = update(step, even, [(step, even)], add=False)

    def pair(_, carry):
        norm, norm_next = carry
        product, _ = apply(even, odd, wide(norm_next / norm))
        first_step = wide(norm_next / product)
        norm, norm_next = norm_next, update(first_step, resid, [])
        product, _ = apply(odd, even, wide(norm_next / norm))
        step = wide(norm_next / product)
        return norm_next, update(step, resid, [(first_step, odd), (step, even)])

    norm, norm_next = lax.fori_loop(0, (ITERS - 2) // 2, pair, (norm, norm_next))
    product, _ = apply(even, odd, wide(norm_next / norm), last=True)
    update(None, None, [(wide(norm_next / product), odd)], norm=False)


def solve_kernel(
    base_in, weight_in, wall, products, jumps, lifts, lines_in, columns,
    out, own_disp,
    disp, resid, search_a, search_b, image, diag, picked, flux, lines, base, weight, in_sem,
):
    pairs = [(lines_in, lines), (base_in, base), (weight_in, weight)]
    local = [pltpu.make_async_copy(a, b, in_sem.at[i]) for i, (a, b) in enumerate(pairs)]
    for copy in local:
        copy.start()
    for copy in local:
        copy.wait()
    solve_wall(wall, disp, resid, (search_a, search_b), image, diag)
    sec, dom = lax.axis_index("sec"), lax.axis_index("dom")
    line = (sec % NC) * NY + sec // NC
    for c in range(3):
        for i in range(8):
            own_disp[c, pl.ds(i, 1), :] = disp[pl.ds((c * T + dom * 8 + i) * 8 + line, 1), :]

    def pick(e, carry):
        at = lines[0, e]
        for c in range(3):
            picked[c, pl.ds(e, 1), :] = disp[pl.ds(c * T * 8 + at, 1), :]
        return carry

    lax.fori_loop(0, NE, pick, 0, unroll=32)
    geometry = []
    for k in range(4):
        row = base[pl.ds(k, 1), :]
        if k < 3:
            found = []
            for start in range(0, NE, 128):
                turned = jnp.transpose(picked[k, pl.ds(start, 128), :])
                chosen = jnp.where(columns[:, pl.ds(start, 128)] != 0.0, turned, 0.0)
                found.append(jnp.sum(chosen, axis=0, keepdims=True))
            row = row * jnp.exp(weight[...] * jnp.concatenate(found, axis=1))
        geometry.append(row)
    for face in range(6):
        at = pl.ds(face * 128, 128)
        flux[at, :] = (geometry[face // 2] * jumps[at, :]).astype(BF16)
    result = dot(lifts[...], flux[...])
    for k in range(4):
        result = result + geometry[k] * products[k]
    out[...] = result.astype(BF16)


def on_device(
    flow_state, base_geometry, anchor_weight, wall_anchor, face_nbr, volume_ops, lift_ops, face_jac, wall_load, wall_stiff
):
    wall, *prepared = exchange(
        wall_load, wall_stiff, flow_state, face_nbr, wall_anchor, volume_ops, lift_ops, face_jac
    )
    wall = wall.reshape(3 * T * 9, 128)
    vmem = pl.BlockSpec(memory_space=pltpu.VMEM)
    far = pl.BlockSpec(memory_space=pltpu.HBM)
    field = pltpu.VMEM((3 * T * 8, 128), F32)
    return pl.pallas_call(
        solve_kernel,
        out_shape=(
            jax.ShapeDtypeStruct((NQ, NE), BF16),
            jax.ShapeDtypeStruct((3, 8, 128), F32),
        ),
        in_specs=[far] * 2 + [vmem] * 6,
        out_specs=(vmem, vmem),
        scratch_shapes=[field] * 6
        + [
            pltpu.VMEM((3, NE, 128), F32),
            pltpu.VMEM((768, NE), BF16),
            pltpu.SMEM((1, NE), jnp.int32),
            pltpu.VMEM((4, NE), F32),
            pltpu.VMEM((1, NE), F32),
            pltpu.SemaphoreType.DMA((3,)),
        ],
        compiler_params=pltpu.CompilerParams(vmem_limit_bytes=28 << 20),
        name="solve",
    )(
        *map(stay, (base_geometry, anchor_weight.reshape(1, NE))), wall, *prepared
    )


def solution(mesh):
    return jax.shard_map(
        on_device,
        mesh=mesh,
        in_specs=(
            P(None, ("sec", "dom")),
            P(None, ("sec", "dom")),
            P(("sec", "dom")),
            P(("sec", "dom")),
            P(None, ("sec", "dom")),
            P(),
            P(),
            P(),
            P(None, ("sec", "dom"), None),
            P(None, ("sec", "dom"), None),
        ),
        out_specs=(P(None, ("sec", "dom")), P(None, ("sec", "dom"), None)),
        check_vma=False,
    )
```

```python
import jax
import jax.numpy as jnp
import numpy as np
from jax import lax
from jax.experimental import pallas as pl
from jax.experimental.pallas import tpu as pltpu
from jax.sharding import PartitionSpec as P

MESH = pl.DeviceIdType.MESH
ITERS = 8
NQ = 270
NF = 90
NE = 1024
HB = 128
NY, NC, NX, NZ = 4, 2, 4, 8
SIZE = {"y": NY, "x": NX, "z": NZ}
ORDERS = (("z", "x", "y"), ("x", "y", "z"), ("z", "y", "x"))
SLOTS = 24
T = 256
UNROLL = 256
BUNROLL = 64
STIFF_LOW, STIFF_UNIT = 0.01, 0.29 / 65535.0
F32 = jnp.float32
BF16 = jnp.bfloat16


def selection():
    index = np.arange(NQ).reshape(5, 2, 3, 3, 3)
    rows = np.zeros((6, 128, NQ), np.float32)
    for face in range(6):
        picked = np.take(index, 0 if face % 2 == 0 else 2, axis=2 + face // 2).reshape(-1)
        rows[face, np.arange(NF), picked] = 1.0
    return rows


def expansion():
    inside, entry = np.arange(NF), np.arange(25)
    down = np.zeros((128, 128), np.float32)
    down[:NF, :25] = inside[:, None] // 18 == entry[None, :] // 5
    across = np.zeros((128, 128), np.float32)
    across[:25, :NF] = entry[:, None] % 5 == inside[None, :] // 18
    same = np.zeros((128, 128), np.float32)
    same[:NF, :NF] = inside[:, None] % 18 == inside[None, :] % 18
    return down, across, same


def coordinates():
    sec, dom = lax.axis_index("sec"), lax.axis_index("dom")
    return {"y": sec // NC, "core": sec % NC, "x": dom // NZ, "z": dom % NZ}


def device(place):
    return (place["y"] * NC + place["core"], place["x"] * NZ + place["z"])


def moved(place, axis, by):
    size = SIZE[axis]
    return dict(place, **{axis: (place[axis] + by + size) % size})


class Gather:
    def __init__(self, color, here, wall, send, recv, pass_send, pass_recv):
        self.color, self.here, self.wall = color, here, wall
        self.sems, self.pass_sems = (send, recv), (pass_send, pass_recv)
        self.order = ORDERS[color]
        self.size = SIZE[self.order[2]]
        self.reach = self.size // 2
        self.events = 4 + 2 * (self.reach - 1)
        self.lines, self.ring, self.passed = [[], []], {}, []
        self.used = 0

    def block(self, stage, axis, at, half):
        index = {}
        for name in "yxz":
            if name in self.order[:stage]:
                index[name] = slice(None)
            elif name == axis:
                index[name] = at
            else:
                index[name] = self.here[name]
        if half is not None:
            cut = "x" if axis != "x" else "z"
            index[cut] = pl.ds(half * (SIZE[cut] // 2), SIZE[cut] // 2)
        core = self.here["core"]
        if isinstance(index["y"], slice):
            line = pl.ds(pl.multiple_of(core * NY, NY), NY)
        else:
            line = core * NY + index["y"]
        return self.wall.at[self.color, index["x"], index["z"], :, line]

    def copy(self, stage, axis, at, half, target, sems, slot):
        source = self.block(stage, axis, at, half)
        copy = pltpu.make_async_remote_copy(
            src_ref=source,
            dst_ref=source,
            send_sem=sems[0].at[slot],
            recv_sem=sems[1].at[slot],
            device_id=device(target),
            device_id_type=MESH,
        )
        copy.start()
        return copy

    def slot(self):
        self.used += 1
        return self.color * SLOTS + self.used - 1

    def launch_line(self, number):
        axis = self.order[number]
        for by in sorted(range(1, SIZE[axis]), key=lambda by: -min(by, SIZE[axis] - by)):
            target = moved(self.here, axis, by)
            self.lines[number].append(
                self.copy(number, axis, self.here[axis], None, target, self.sems, self.slot())
            )

    def around(self, by):
        return (self.here[self.order[2]] + by + self.size) % self.size

    def launch_ring(self, step, half):
        for way, sign in enumerate((1, -1)):
            if step == self.reach - 1 and way != half:
                continue
            target = moved(self.here, self.order[2], sign)
            self.ring[step, half, way] = self.copy(
                2, self.order[2], self.around(-sign * step), half, target, self.sems, self.slot()
            )

    def hand_over(self, by, half):
        slot = self.color * 2 * NZ + len(self.passed)
        partner = dict(self.here, core=1 - self.here["core"])
        self.passed.append(self.copy(2, self.order[2], self.around(by), half, partner, self.pass_sems, slot))

    def advance(self, event):
        if event >= self.events:
            return
        if event < 2:
            if event == 1:
                for copy in self.lines[0]:
                    copy.wait_recv()
            self.launch_line(event)
        elif event == 2:
            for copy in self.lines[1]:
                copy.wait_recv()
            self.launch_ring(0, 0)
            self.launch_ring(0, 1)
            self.hand_over(0, 0)
            self.hand_over(0, 1)
        elif event < self.events - 1:
            step, half = (event - 3) // 2 + 1, (event - 3) % 2
            for way in range(2):
                self.ring[step - 1, half, way].wait_recv()
            self.launch_ring(step, half)
            self.hand_over(-step, half)
            self.hand_over(step, half)
        else:
            for half in range(2):
                self.ring[self.reach - 1, half, half].wait_recv()
                self.hand_over(self.reach, half)

    def finish(self):
        for copy in self.lines[0] + self.lines[1] + list(self.ring.values()):
            copy.wait_send()
        for copy in self.passed:
            copy.wait()


def dot(a, b):
    return jnp.dot(a, b, preferred_element_type=F32)


def pack_wall(load, stiff, out):
    largest = jnp.max(jnp.max(jnp.abs(load), axis=0, keepdims=True), axis=1, keepdims=True)
    power = jnp.ceil(jnp.log2(jnp.maximum(largest, 1e-30)) + 1e-4)
    power = jnp.broadcast_to(power, (1, 128)).astype(jnp.int32)
    unit = load_unit(power)
    high = jnp.clip(jnp.round(load / unit), -32767.0, 32767.0).astype(jnp.int32)
    low = jnp.clip(jnp.round((stiff - STIFF_LOW) / STIFF_UNIT), 0.0, 65535.0).astype(jnp.int32)
    word = (high << 16) | low
    for i in range(8):
        out[pl.ds(i, 1), :] = word[i : i + 1]
    out[pl.ds(8, 1), :] = power


def load_unit(power):
    return jnp.exp2(power.astype(F32)) * (1.0 / 32767.0)


def find_anchors(anchor, lines, columns):
    place = anchor[...]
    section = place >> 15
    lines[...] = ((place >> 7) & (T - 1)) * 8 + (section & 1) * NY + (section >> 1)
    column = lax.broadcasted_iota(jnp.int32, (128, 1), 0)
    columns[...] = jnp.where(column == (place & 127), 1.0, 0.0)


def volume_part(direction, flow, vol, products):
    products[direction] = dot(vol[:, direction, :], flow[...])


def flux_entries(jac, table, entries):
    table[...] = jnp.zeros_like(table)
    for v in range(5):
        for w in range(5):
            both = jac[v, w].astype(F32)
            for side in range(2):
                table[side, pl.ds(v * 5 + w, 1), pl.ds(0, 6)] = both[side : side + 1]
    for side in range(2):
        entries[side] = jnp.transpose(table[side])


def face_part(face, flow, heads, nbr, entries, sel, down, across, same, jumps, cand):
    state = flow[...]
    row = lax.broadcasted_iota(jnp.int32, (256, 1), 0).astype(F32).astype(BF16)
    other = sel[face ^ 1]
    cand[:, pl.ds(0, NE)] = dot(other, state).astype(BF16)
    width = NE
    if face < 4:
        cand[:, pl.ds(NE, HB)] = dot(other, heads[face]).astype(BF16)
        width = NE + HB
    place = nbr[pl.ds(face, 1), :]
    theirs = jnp.zeros((128, NE), F32)
    for start in range(0, width, 256):
        size = min(256, width - start)
        key = jnp.where((place >= start) & (place < start + size), place - start, -1)
        key = key.astype(F32).astype(BF16)
        chosen = jnp.where(row[:size] == key, jnp.ones((), BF16), jnp.zeros((), BF16))
        theirs = theirs + dot(cand[:, pl.ds(start, size)], chosen)
    mine = dot(sel[face], state)
    mixes = []
    for side in range(2):
        tall = (down[...] * entries[side, pl.ds(face, 1), :]).astype(BF16)
        wide = dot(tall, across[...])
        mixes.append((wide * same[...]).astype(BF16))
    jumps[pl.ds(face * 128, 128), :] = dot(mixes[0], mine.astype(BF16)) + dot(mixes[1], theirs.astype(BF16))


def exchange_kernel(
    load, stiff, flow_in, nbr_in, anchor_in, vol_in, lift_in, jac_in, sel_in, down_in, across_in, same_in,
    wall, products, jumps, lifts, lines, columns,
    heads, flow, nbr, anchor, vol, lift, jac, sel, down, across, same, table, entries, cand, own_load, own_stiff,
    send, recv, pass_send, pass_recv, head_send, head_recv, in_sem,
):
    here = coordinates()
    sec, dom = lax.axis_index("sec"), lax.axis_index("dom")
    n_sec, n_dom = NY * NC, NX * NZ
    sides = [
        (sec, (dom + 1) % n_dom),
        (sec, (dom + n_dom - 1) % n_dom),
        ((sec + 1) % n_sec, dom),
        ((sec + n_sec - 1) % n_sec, dom),
    ]
    peers = list(sides)
    for axis in "yxz":
        for by in range(1, SIZE[axis]):
            peers.append(device(moved(here, axis, by)))
    peers.append(device(dict(here, core=1 - here["core"])))
    barrier = pltpu.get_barrier_semaphore()
    for peer in peers:
        pl.semaphore_signal(barrier, inc=1, device_id=peer, device_id_type=MESH)
    pairs = [
        (load, own_load), (stiff, own_stiff), (flow_in, flow), (nbr_in, nbr), (anchor_in, anchor),
        (vol_in, vol), (jac_in, jac),
        (sel_in, sel), (down_in, down), (across_in, across), (same_in, same), (lift_in, lift),
    ]
    local = [pltpu.make_async_copy(a, b, in_sem.at[i]) for i, (a, b) in enumerate(pairs)]
    for copy in local:
        copy.start()
    local[0].wait()
    local[1].wait()
    line = here["core"] * NY + here["y"]
    for c in range(3):
        pack_wall(own_load[c], own_stiff[c], wall.at[c, here["x"], here["z"], :, line])
    lifts[...] = jnp.zeros_like(lifts)
    pl.semaphore_wait(barrier, len(peers))
    gathers = [Gather(color, here, wall, send, recv, pass_send, pass_recv) for color in range(3)]

    def advance(*pairs):
        for color, event in pairs:
            gathers[color].advance(event)

    def face(number):
        face_part(number, flow, heads, nbr, entries, sel, down, across, same, jumps, cand)

    advance((1, 0), (0, 0), (2, 0))
    head_copies = []
    for number, peer in enumerate(sides):
        copy = pltpu.make_async_remote_copy(
            src_ref=flow_in.at[:, pl.ds(0, HB)],
            dst_ref=heads.at[number],
            send_sem=head_send.at[number],
            recv_sem=head_recv.at[number],
            device_id=peer,
            device_id_type=MESH,
        )
        copy.start()
        head_copies.append(copy)
    for copy in local[2:]:
        copy.wait()
    for direction in range(2):
        volume_part(direction, flow, vol, products)
    advance((1, 1), (0, 1), (2, 1))
    for direction in range(2, 4):
        volume_part(direction, flow, vol, products)
    flux_entries(jac, table, entries)
    find_anchors(anchor, lines, columns)
    for number in range(6):
        lifts[:, pl.ds(number * 128, NF)] = lift[number]
    face(4)
    face(5)
    advance((1, 2), (0, 2), (2, 2))
    for copy in head_copies:
        copy.wait()
    face(0)
    advance((1, 3), (1, 4), (0, 3), (2, 3))
    face(1)
    advance((1, 5), (1, 6), (0, 4), (2, 4))
    face(2)
    advance((1, 7), (1, 8), (0, 5), (2, 5))
    face(3)
    advance((1, 9),)
    for gather in gathers:
        gather.finish()


def stay(x):
    return pltpu.with_memory_space_constraint(x, pltpu.HBM)


def exchange(wall_load, wall_stiff, flow_state, face_nbr, wall_anchor, volume_ops, lift_ops, face_jac):
    vmem = pl.BlockSpec(memory_space=pltpu.VMEM)
    far = pl.BlockSpec(memory_space=pltpu.HBM)
    down, across, same = expansion()
    dma = pltpu.SemaphoreType.DMA
    return pl.pallas_call(
        exchange_kernel,
        out_shape=(
            jax.ShapeDtypeStruct((3, NX, NZ, 9, NC * NY, 128), jnp.int32),
            jax.ShapeDtypeStruct((4, NQ, NE), F32),
            jax.ShapeDtypeStruct((768, NE), F32),
            jax.ShapeDtypeStruct((NQ, 768), BF16),
            jax.ShapeDtypeStruct((1, NE), jnp.int32),
            jax.ShapeDtypeStruct((128, NE), F32),
        ),
        in_specs=[far] * 12,
        out_specs=(vmem,) * 6,
        scratch_shapes=[
            pltpu.VMEM((4, NQ, HB), BF16),
            pltpu.VMEM((NQ, NE), BF16),
            pltpu.VMEM((6, NE), jnp.int32),
            pltpu.VMEM((1, NE), jnp.int32),
            pltpu.VMEM((NQ, 4, NQ), BF16),
            pltpu.VMEM((6, NQ, NF), BF16),
            pltpu.VMEM((5, 5, 2, 6), BF16),
            pltpu.VMEM((6, 128, NQ), BF16),
            pltpu.VMEM((128, 128), F32),
            pltpu.VMEM((128, 128), BF16),
            pltpu.VMEM((128, 128), F32),
            pltpu.VMEM((2, 128, 128), F32),
            pltpu.VMEM((2, 128, 128), F32),
            pltpu.VMEM((128, NE + HB), BF16),
            pltpu.VMEM((3, 8, 128), F32),
            pltpu.VMEM((3, 8, 128), F32),
            dma((3 * SLOTS,)),
            dma((3 * SLOTS,)),
            dma((3 * 2 * NZ,)),
            dma((3 * 2 * NZ,)),
            dma((4,)),
            dma((4,)),
            dma((12,)),
        ],
        compiler_params=pltpu.CompilerParams(collective_id=0, has_side_effects=True, vmem_limit_bytes=32 << 20),
        name="exchange",
    )(
        *map(
            stay,
            (
                wall_load, wall_stiff, flow_state, face_nbr, wall_anchor.reshape(1, NE),
                jnp.transpose(volume_ops, (1, 0, 2)), lift_ops, jnp.transpose(face_jac, (2, 3, 1, 0)),
                jnp.asarray(selection(), BF16), jnp.asarray(down, F32), jnp.asarray(across, BF16),
                jnp.asarray(same, F32),
            ),
        )
    )


def rows(i):
    return pl.ds(pl.multiple_of(i * 8, 8), 8)


def solve_wall(wall, disp, resid, searches, image, diag):
    lane = lax.broadcasted_iota(jnp.int32, (8, 128), 1)
    sub = lax.broadcasted_iota(jnp.int32, (8, 128), 0)
    zero = jnp.zeros((8, 128), F32)

    def total(acc):
        return jnp.sum(jnp.sum(acc, axis=0, keepdims=True), axis=1, keepdims=True)

    def wide(value):
        return jnp.broadcast_to(value, (8, 128))

    def previous(v):
        return jnp.where(sub >= 4, pltpu.roll(v, 4, 0), jnp.where(sub == 0, 0.0, pltpu.roll(v, 5, 0)))

    def following(v):
        return jnp.where(sub < 4, pltpu.roll(v, 4, 0), jnp.where(sub == 7, 0.0, pltpu.roll(v, 3, 0)))

    def apply(old, new, ratio, first=False, last=False):
        units = {}

        def packed(c, b, u):
            group = (c * T + b * UNROLL) // 8 + u // 8
            return group, wall[rows(group * 9 + u % 8), :]

        def direction(c, b, u):
            if not first:
                i = rows(c * T + b * UNROLL + u)
                return resid[i, :] + ratio * old[i, :]
            group, word = packed(c, b, u)
            if u // 8 not in units:
                units[u // 8] = load_unit(wall[rows(group * 9 + 8), :])
            return (word >> 16).astype(F32) * units[u // 8]

        sums = norms = (zero, zero)
        for c in range(3):
            units.clear()
            top = direction(c, 0, 0)
            units.clear()
            bottom = direction(c, T // UNROLL - 1, UNROLL - 1)

            def block(b, carry, ends=False):
                above, here, sums, norms = carry
                units.clear()
                for u in range(UNROLL):
                    i = rows(c * T + b * UNROLL + u)
                    below = following(top) if ends and u == UNROLL - 1 else direction(c, b, u + 1)
                    left = jnp.where(lane == 0, 0.0, pltpu.roll(here, 1, 1))
                    right = jnp.where(lane == 127, 0.0, pltpu.roll(here, 127, 1))
                    if first:
                        code = packed(c, b, u)[1] & 65535
                        middle = (4.0 + STIFF_LOW) + code.astype(F32) * STIFF_UNIT
                        diag[i, :] = middle
                        norms = (norms[1], norms[0] + here * here)
                    else:
                        middle = diag[i, :]
                    value = middle * here - ((above + below) + (left + right))
                    if not last:
                        image[i, :] = value
                    new[i, :] = here
                    sums = (sums[1], sums[0] + here * value)
                    above, here = here, below
                return above, here, sums, norms

            carry = (previous(bottom), top, sums, norms)
            if T > UNROLL:
                carry = lax.fori_loop(0, T // UNROLL - 1, block, carry)
            _, _, sums, norms = block(T // UNROLL - 1, carry, ends=True)
        return total(sums[0] + sums[1]), total(norms[0] + norms[1]) if first else None

    def update(step, source, moves, add=True, norm=True):
        def block(b, norms):
            for u in range(BUNROLL):
                i = rows(b * BUNROLL + u)
                if moves:
                    gain = moves[0][0] * moves[0][1][i, :]
                    for size, field in moves[1:]:
                        gain = gain + size * field[i, :]
                    disp[i, :] = disp[i, :] + gain if add else gain
                if norm:
                    held = source[i, :] - step * image[i, :]
                    resid[i, :] = held
                    norms = (norms[1], norms[0] + held * held)
            return norms

        norms = lax.fori_loop(0, 3 * T // BUNROLL, block, (zero, zero))
        return total(norms[0] + norms[1]) if norm else None

    even, odd = searches
    product, norm = apply(None, even, None, first=True)
    step = wide(norm / product)
    norm_next = update(step, even, [(step, even)], add=False)

    def pair(_, carry):
        norm, norm_next = carry
        product, _ = apply(even, odd, wide(norm_next / norm))
        first_step = wide(norm_next / product)
        norm, norm_next = norm_next, update(first_step, resid, [])
        product, _ = apply(odd, even, wide(norm_next / norm))
        step = wide(norm_next / product)
        return norm_next, update(step, resid, [(first_step, odd), (step, even)])

    norm, norm_next = lax.fori_loop(0, (ITERS - 2) // 2, pair, (norm, norm_next))
    product, _ = apply(even, odd, wide(norm_next / norm), last=True)
    update(None, None, [(wide(norm_next / product), odd)], norm=False)


def solve_kernel(
    base_in, weight_in, wall, products, jumps, lifts, lines_in, columns,
    out, own_disp,
    disp, resid, search_a, search_b, image, diag, picked, flux, lines, base, weight, in_sem,
):
    pairs = [(lines_in, lines), (base_in, base), (weight_in, weight)]
    local = [pltpu.make_async_copy(a, b, in_sem.at[i]) for i, (a, b) in enumerate(pairs)]
    for copy in local:
        copy.start()
    for copy in local:
        copy.wait()
    solve_wall(wall, disp, resid, (search_a, search_b), image, diag)
    sec, dom = lax.axis_index("sec"), lax.axis_index("dom")
    line = (sec % NC) * NY + sec // NC
    for c in range(3):
        for i in range(8):
            own_disp[c, pl.ds(i, 1), :] = disp[pl.ds((c * T + dom * 8 + i) * 8 + line, 1), :]

    def pick(e, carry):
        at = lines[0, e]
        for c in range(3):
            picked[c, pl.ds(e, 1), :] = disp[pl.ds(c * T * 8 + at, 1), :]
        return carry

    lax.fori_loop(0, NE, pick, 0, unroll=32)
    geometry = []
    for k in range(4):
        row = base[pl.ds(k, 1), :]
        if k < 3:
            found = []
            for start in range(0, NE, 128):
                turned = jnp.transpose(picked[k, pl.ds(start, 128), :])
                chosen = jnp.where(columns[:, pl.ds(start, 128)] != 0.0, turned, 0.0)
                found.append(jnp.sum(chosen, axis=0, keepdims=True))
            row = row * jnp.exp(weight[...] * jnp.concatenate(found, axis=1))
        geometry.append(row)
    for face in range(6):
        at = pl.ds(face * 128, 128)
        flux[at, :] = (geometry[face // 2] * jumps[at, :]).astype(BF16)
    result = dot(lifts[...], flux[...])
    for k in range(4):
        result = result + geometry[k] * products[k]
    out[...] = result.astype(BF16)


def on_device(
    flow_state, base_geometry, anchor_weight, wall_anchor, face_nbr, volume_ops, lift_ops, face_jac, wall_load, wall_stiff
):
    wall, *prepared = exchange(
        wall_load, wall_stiff, flow_state, face_nbr, wall_anchor, volume_ops, lift_ops, face_jac
    )
    wall = wall.reshape(3 * T * 9, 128)
    vmem = pl.BlockSpec(memory_space=pltpu.VMEM)
    far = pl.BlockSpec(memory_space=pltpu.HBM)
    field = pltpu.VMEM((3 * T * 8, 128), F32)
    return pl.pallas_call(
        solve_kernel,
        out_shape=(
            jax.ShapeDtypeStruct((NQ, NE), BF16),
            jax.ShapeDtypeStruct((3, 8, 128), F32),
        ),
        in_specs=[far] * 2 + [vmem] * 6,
        out_specs=(vmem, vmem),
        scratch_shapes=[field] * 6
        + [
            pltpu.VMEM((3, NE, 128), F32),
            pltpu.VMEM((768, NE), BF16),
            pltpu.SMEM((1, NE), jnp.int32),
            pltpu.VMEM((4, NE), F32),
            pltpu.VMEM((1, NE), F32),
            pltpu.SemaphoreType.DMA((3,)),
        ],
        compiler_params=pltpu.CompilerParams(vmem_limit_bytes=28 << 20),
        name="solve",
    )(
        *map(stay, (base_geometry, anchor_weight.reshape(1, NE))), wall, *prepared
    )


def solution(mesh):
    return jax.shard_map(
        on_device,
        mesh=mesh,
        in_specs=(
            P(None, ("sec", "dom")),
            P(None, ("sec", "dom")),
            P(("sec", "dom")),
            P(("sec", "dom")),
            P(None, ("sec", "dom")),
            P(),
            P(),
            P(),
            P(None, ("sec", "dom"), None),
            P(None, ("sec", "dom"), None),
        ),
        out_specs=(P(None, ("sec", "dom")), P(None, ("sec", "dom"), None)),
        check_vma=False,
    )
```

```python
import jax
import jax.numpy as jnp
import numpy as np
from jax import lax
from jax.experimental import pallas as pl
from jax.experimental.pallas import tpu as pltpu
from jax.sharding import PartitionSpec as P

MESH = pl.DeviceIdType.MESH
ITERS = 8
NQ = 270
NF = 90
NE = 1024
HB = 128
NY, NC, NX, NZ = 4, 2, 4, 8
SIZE = {"y": NY, "x": NX, "z": NZ}
ORDERS = (("z", "x", "y"), ("x", "y", "z"), ("z", "y", "x"))
SLOTS = 24
T = 256
UNROLL = 256
BUNROLL = 64
STIFF_LOW, STIFF_UNIT = 0.01, 0.29 / 65535.0
F32 = jnp.float32
BF16 = jnp.bfloat16


def selection():
    index = np.arange(NQ).reshape(5, 2, 3, 3, 3)
    rows = np.zeros((6, 128, NQ), np.float32)
    for face in range(6):
        picked = np.take(index, 0 if face % 2 == 0 else 2, axis=2 + face // 2).reshape(-1)
        rows[face, np.arange(NF), picked] = 1.0
    return rows


def expansion():
    inside, entry = np.arange(NF), np.arange(25)
    down = np.zeros((128, 128), np.float32)
    down[:NF, :25] = inside[:, None] // 18 == entry[None, :] // 5
    across = np.zeros((128, 128), np.float32)
    across[:25, :NF] = entry[:, None] % 5 == inside[None, :] // 18
    same = np.zeros((128, 128), np.float32)
    same[:NF, :NF] = inside[:, None] % 18 == inside[None, :] % 18
    return down, across, same


def coordinates():
    sec, dom = lax.axis_index("sec"), lax.axis_index("dom")
    return {"y": sec // NC, "core": sec % NC, "x": dom // NZ, "z": dom % NZ}


def device(place):
    return (place["y"] * NC + place["core"], place["x"] * NZ + place["z"])


def moved(place, axis, by):
    size = SIZE[axis]
    return dict(place, **{axis: (place[axis] + by + size) % size})


class Gather:
    def __init__(self, color, here, wall, send, recv, pass_send, pass_recv):
        self.color, self.here, self.wall = color, here, wall
        self.sems, self.pass_sems = (send, recv), (pass_send, pass_recv)
        self.order = ORDERS[color]
        self.size = SIZE[self.order[2]]
        self.reach = self.size // 2
        self.events = 4 + 2 * (self.reach - 1)
        self.lines, self.ring, self.passed = [[], []], {}, []
        self.used = 0

    def block(self, stage, axis, at, half):
        index = {}
        for name in "yxz":
            if name in self.order[:stage]:
                index[name] = slice(None)
            elif name == axis:
                index[name] = at
            else:
                index[name] = self.here[name]
        if half is not None:
            cut = "x" if axis != "x" else "z"
            index[cut] = pl.ds(half * (SIZE[cut] // 2), SIZE[cut] // 2)
        core = self.here["core"]
        if isinstance(index["y"], slice):
            line = pl.ds(pl.multiple_of(core * NY, NY), NY)
        else:
            line = core * NY + index["y"]
        return self.wall.at[self.color, index["x"], index["z"], :, line]

    def copy(self, stage, axis, at, half, target, sems, slot):
        source = self.block(stage, axis, at, half)
        copy = pltpu.make_async_remote_copy(
            src_ref=source,
            dst_ref=source,
            send_sem=sems[0].at[slot],
            recv_sem=sems[1].at[slot],
            device_id=device(target),
            device_id_type=MESH,
        )
        copy.start()
        return copy

    def slot(self):
        self.used += 1
        return self.color * SLOTS + self.used - 1

    def launch_line(self, number):
        axis = self.order[number]
        for by in sorted(range(1, SIZE[axis]), key=lambda by: -min(by, SIZE[axis] - by)):
            target = moved(self.here, axis, by)
            self.lines[number].append(
                self.copy(number, axis, self.here[axis], None, target, self.sems, self.slot())
            )

    def around(self, by):
        return (self.here[self.order[2]] + by + self.size) % self.size

    def launch_ring(self, step, half):
        for way, sign in enumerate((1, -1)):
            if step == self.reach - 1 and way != half:
                continue
            target = moved(self.here, self.order[2], sign)
            self.ring[step, half, way] = self.copy(
                2, self.order[2], self.around(-sign * step), half, target, self.sems, self.slot()
            )

    def hand_over(self, by, half):
        slot = self.color * 2 * NZ + len(self.passed)
        partner = dict(self.here, core=1 - self.here["core"])
        self.passed.append(self.copy(2, self.order[2], self.around(by), half, partner, self.pass_sems, slot))

    def advance(self, event):
        if event >= self.events:
            return
        if event < 2:
            if event == 1:
                for copy in self.lines[0]:
                    copy.wait_recv()
            self.launch_line(event)
        elif event == 2:
            for copy in self.lines[1]:
                copy.wait_recv()
            self.launch_ring(0, 0)
            self.launch_ring(0, 1)
            self.hand_over(0, 0)
            self.hand_over(0, 1)
        elif event < self.events - 1:
            step, half = (event - 3) // 2 + 1, (event - 3) % 2
            for way in range(2):
                self.ring[step - 1, half, way].wait_recv()
            self.launch_ring(step, half)
            self.hand_over(-step, half)
            self.hand_over(step, half)
        else:
            for half in range(2):
                self.ring[self.reach - 1, half, half].wait_recv()
                self.hand_over(self.reach, half)

    def finish(self):
        for copy in self.lines[0] + self.lines[1] + list(self.ring.values()):
            copy.wait_send()
        for copy in self.passed:
            copy.wait()


def dot(a, b):
    return jnp.dot(a, b, preferred_element_type=F32)


def pack_wall(load, stiff, out):
    largest = jnp.max(jnp.max(jnp.abs(load), axis=0, keepdims=True), axis=1, keepdims=True)
    power = jnp.ceil(jnp.log2(jnp.maximum(largest, 1e-30)) + 1e-4)
    power = jnp.broadcast_to(power, (1, 128)).astype(jnp.int32)
    unit = load_unit(power)
    high = jnp.clip(jnp.round(load / unit), -32767.0, 32767.0).astype(jnp.int32)
    low = jnp.clip(jnp.round((stiff - STIFF_LOW) / STIFF_UNIT), 0.0, 65535.0).astype(jnp.int32)
    word = (high << 16) | low
    for i in range(8):
        out[pl.ds(i, 1), :] = word[i : i + 1]
    out[pl.ds(8, 1), :] = power


def load_unit(power):
    return jnp.exp2(power.astype(F32)) * (1.0 / 32767.0)


def find_anchors(anchor, lines, columns):
    place = anchor[...]
    section = place >> 15
    lines[...] = ((place >> 7) & (T - 1)) * 8 + (section & 1) * NY + (section >> 1)
    column = lax.broadcasted_iota(jnp.int32, (128, 1), 0)
    columns[...] = jnp.where(column == (place & 127), 1.0, 0.0)


def volume_part(direction, flow, vol, products):
    products[direction] = dot(vol[:, direction, :], flow[...])


def flux_entries(jac, table, entries):
    table[...] = jnp.zeros_like(table)
    for v in range(5):
        for w in range(5):
            both = jac[v, w].astype(F32)
            for side in range(2):
                table[side, pl.ds(v * 5 + w, 1), pl.ds(0, 6)] = both[side : side + 1]
    for side in range(2):
        entries[side] = jnp.transpose(table[side])


def face_part(face, flow, heads, nbr, entries, sel, down, across, same, jumps, cand):
    state = flow[...]
    row = lax.broadcasted_iota(jnp.int32, (256, 1), 0).astype(F32).astype(BF16)
    other = sel[face ^ 1]
    cand[:, pl.ds(0, NE)] = dot(other, state).astype(BF16)
    width = NE
    if face < 4:
        cand[:, pl.ds(NE, HB)] = dot(other, heads[face]).astype(BF16)
        width = NE + HB
    place = nbr[pl.ds(face, 1), :]
    theirs = jnp.zeros((128, NE), F32)
    for start in range(0, width, 256):
        size = min(256, width - start)
        key = jnp.where((place >= start) & (place < start + size), place - start, -1)
        key = key.astype(F32).astype(BF16)
        chosen = jnp.where(row[:size] == key, jnp.ones((), BF16), jnp.zeros((), BF16))
        theirs = theirs + dot(cand[:, pl.ds(start, size)], chosen)
    mine = dot(sel[face], state)
    mixes = []
    for side in range(2):
        tall = (down[...] * entries[side, pl.ds(face, 1), :]).astype(BF16)
        wide = dot(tall, across[...])
        mixes.append((wide * same[...]).astype(BF16))
    jumps[pl.ds(face * 128, 128), :] = dot(mixes[0], mine.astype(BF16)) + dot(mixes[1], theirs.astype(BF16))


def exchange_kernel(
    load, stiff, flow_in, nbr_in, anchor_in, vol_in, lift_in, jac_in, sel_in, down_in, across_in, same_in,
    wall, products, jumps, lifts, lines, columns,
    heads, flow, nbr, anchor, vol, lift, jac, sel, down, across, same, table, entries, cand, own_load, own_stiff,
    send, recv, pass_send, pass_recv, head_send, head_recv, in_sem,
):
    here = coordinates()
    sec, dom = lax.axis_index("sec"), lax.axis_index("dom")
    n_sec, n_dom = NY * NC, NX * NZ
    sides = [
        (sec, (dom + 1) % n_dom),
        (sec, (dom + n_dom - 1) % n_dom),
        ((sec + 1) % n_sec, dom),
        ((sec + n_sec - 1) % n_sec, dom),
    ]
    peers = list(sides)
    for axis in "yxz":
        for by in range(1, SIZE[axis]):
            peers.append(device(moved(here, axis, by)))
    peers.append(device(dict(here, core=1 - here["core"])))
    barrier = pltpu.get_barrier_semaphore()
    for peer in peers:
        pl.semaphore_signal(barrier, inc=1, device_id=peer, device_id_type=MESH)
    pairs = [
        (load, own_load), (stiff, own_stiff), (flow_in, flow), (nbr_in, nbr), (anchor_in, anchor),
        (vol_in, vol), (jac_in, jac),
        (sel_in, sel), (down_in, down), (across_in, across), (same_in, same), (lift_in, lift),
    ]
    local = [pltpu.make_async_copy(a, b, in_sem.at[i]) for i, (a, b) in enumerate(pairs)]
    for copy in local:
        copy.start()
    local[0].wait()
    local[1].wait()
    line = here["core"] * NY + here["y"]
    for c in range(3):
        pack_wall(own_load[c], own_stiff[c], wall.at[c, here["x"], here["z"], :, line])
    lifts[...] = jnp.zeros_like(lifts)
    pl.semaphore_wait(barrier, len(peers))
    gathers = [Gather(color, here, wall, send, recv, pass_send, pass_recv) for color in range(3)]

    def advance(*pairs):
        for color, event in pairs:
            gathers[color].advance(event)

    def face(number):
        face_part(number, flow, heads, nbr, entries, sel, down, across, same, jumps, cand)

    advance((1, 0), (0, 0), (2, 0))
    head_copies = []
    for number, peer in enumerate(sides):
        copy = pltpu.make_async_remote_copy(
            src_ref=flow_in.at[:, pl.ds(0, HB)],
            dst_ref=heads.at[number],
            send_sem=head_send.at[number],
            recv_sem=head_recv.at[number],
            device_id=peer,
            device_id_type=MESH,
        )
        copy.start()
        head_copies.append(copy)
    for copy in local[2:]:
        copy.wait()
    for direction in range(2):
        volume_part(direction, flow, vol, products)
    advance((1, 1), (0, 1), (2, 1))
    for direction in range(2, 4):
        volume_part(direction, flow, vol, products)
    flux_entries(jac, table, entries)
    find_anchors(anchor, lines, columns)
    for number in range(6):
        lifts[:, pl.ds(number * 128, NF)] = lift[number]
    face(4)
    face(5)
    advance((1, 2), (0, 2), (2, 2))
    for copy in head_copies:
        copy.wait()
    face(0)
    advance((1, 3), (1, 4), (0, 3), (2, 3))
    face(1)
    advance((1, 5), (1, 6), (0, 4), (2, 4))
    face(2)
    advance((1, 7), (1, 8), (0, 5), (2, 5))
    face(3)
    advance((1, 9),)
    for gather in gathers:
        gather.finish()


def stay(x):
    return pltpu.with_memory_space_constraint(x, pltpu.HBM)


def exchange(wall_load, wall_stiff, flow_state, face_nbr, wall_anchor, volume_ops, lift_ops, face_jac):
    vmem = pl.BlockSpec(memory_space=pltpu.VMEM)
    far = pl.BlockSpec(memory_space=pltpu.HBM)
    down, across, same = expansion()
    dma = pltpu.SemaphoreType.DMA
    return pl.pallas_call(
        exchange_kernel,
        out_shape=(
            jax.ShapeDtypeStruct((3, NX, NZ, 9, NC * NY, 128), jnp.int32),
            jax.ShapeDtypeStruct((4, NQ, NE), F32),
            jax.ShapeDtypeStruct((768, NE), F32),
            jax.ShapeDtypeStruct((NQ, 768), BF16),
            jax.ShapeDtypeStruct((1, NE), jnp.int32),
            jax.ShapeDtypeStruct((128, NE), F32),
        ),
        in_specs=[far] * 12,
        out_specs=(vmem,) * 6,
        scratch_shapes=[
            pltpu.VMEM((4, NQ, HB), BF16),
            pltpu.VMEM((NQ, NE), BF16),
            pltpu.VMEM((6, NE), jnp.int32),
            pltpu.VMEM((1, NE), jnp.int32),
            pltpu.VMEM((NQ, 4, NQ), BF16),
            pltpu.VMEM((6, NQ, NF), BF16),
            pltpu.VMEM((5, 5, 2, 6), BF16),
            pltpu.VMEM((6, 128, NQ), BF16),
            pltpu.VMEM((128, 128), F32),
            pltpu.VMEM((128, 128), BF16),
            pltpu.VMEM((128, 128), F32),
            pltpu.VMEM((2, 128, 128), F32),
            pltpu.VMEM((2, 128, 128), F32),
            pltpu.VMEM((128, NE + HB), BF16),
            pltpu.VMEM((3, 8, 128), F32),
            pltpu.VMEM((3, 8, 128), F32),
            dma((3 * SLOTS,)),
            dma((3 * SLOTS,)),
            dma((3 * 2 * NZ,)),
            dma((3 * 2 * NZ,)),
            dma((4,)),
            dma((4,)),
            dma((12,)),
        ],
        compiler_params=pltpu.CompilerParams(collective_id=0, has_side_effects=True, vmem_limit_bytes=32 << 20),
        name="exchange",
    )(
        *map(
            stay,
            (
                wall_load, wall_stiff, flow_state, face_nbr, wall_anchor.reshape(1, NE),
                jnp.transpose(volume_ops, (1, 0, 2)), lift_ops, jnp.transpose(face_jac, (2, 3, 1, 0)),
                jnp.asarray(selection(), BF16), jnp.asarray(down, F32), jnp.asarray(across, BF16),
                jnp.asarray(same, F32),
            ),
        )
    )


def rows(i):
    return pl.ds(pl.multiple_of(i * 8, 8), 8)


def solve_wall(wall, disp, resid, searches, image, diag):
    lane = lax.broadcasted_iota(jnp.int32, (8, 128), 1)
    sub = lax.broadcasted_iota(jnp.int32, (8, 128), 0)
    zero = jnp.zeros((8, 128), F32)

    def total(acc):
        return jnp.sum(jnp.sum(acc, axis=0, keepdims=True), axis=1, keepdims=True)

    def wide(value):
        return jnp.broadcast_to(value, (8, 128))

    def previous(v):
        return jnp.where(sub >= 4, pltpu.roll(v, 4, 0), jnp.where(sub == 0, 0.0, pltpu.roll(v, 5, 0)))

    def following(v):
        return jnp.where(sub < 4, pltpu.roll(v, 4, 0), jnp.where(sub == 7, 0.0, pltpu.roll(v, 3, 0)))

    def apply(old, new, ratio, first=False, last=False):
        units = {}

        def packed(c, b, u):
            group = (c * T + b * UNROLL) // 8 + u // 8
            return group, wall[rows(group * 9 + u % 8), :]

        def direction(c, b, u):
            if not first:
                i = rows(c * T + b * UNROLL + u)
                return resid[i, :] + ratio * old[i, :]
            group, word = packed(c, b, u)
            if u // 8 not in units:
                units[u // 8] = load_unit(wall[rows(group * 9 + 8), :])
            return (word >> 16).astype(F32) * units[u // 8]

        sums = norms = (zero, zero)
        for c in range(3):
            units.clear()
            top = direction(c, 0, 0)
            units.clear()
            bottom = direction(c, T // UNROLL - 1, UNROLL - 1)

            def block(b, carry, ends=False):
                above, here, sums, norms = carry
                units.clear()
                for u in range(UNROLL):
                    i = rows(c * T + b * UNROLL + u)
                    below = following(top) if ends and u == UNROLL - 1 else direction(c, b, u + 1)
                    left = jnp.where(lane == 0, 0.0, pltpu.roll(here, 1, 1))
                    right = jnp.where(lane == 127, 0.0, pltpu.roll(here, 127, 1))
                    if first:
                        code = packed(c, b, u)[1] & 65535
                        middle = (4.0 + STIFF_LOW) + code.astype(F32) * STIFF_UNIT
                        diag[i, :] = middle
                        norms = (norms[1], norms[0] + here * here)
                    else:
                        middle = diag[i, :]
                    value = middle * here - ((above + below) + (left + right))
                    if not last:
                        image[i, :] = value
                    new[i, :] = here
                    sums = (sums[1], sums[0] + here * value)
                    above, here = here, below
                return above, here, sums, norms

            carry = (previous(bottom), top, sums, norms)
            if T > UNROLL:
                carry = lax.fori_loop(0, T // UNROLL - 1, block, carry)
            _, _, sums, norms = block(T // UNROLL - 1, carry, ends=True)
        return total(sums[0] + sums[1]), total(norms[0] + norms[1]) if first else None

    def update(step, source, moves, add=True, norm=True):
        def block(b, norms):
            for u in range(BUNROLL):
                i = rows(b * BUNROLL + u)
                if moves:
                    gain = moves[0][0] * moves[0][1][i, :]
                    for size, field in moves[1:]:
                        gain = gain + size * field[i, :]
                    disp[i, :] = disp[i, :] + gain if add else gain
                if norm:
                    held = source[i, :] - step * image[i, :]
                    resid[i, :] = held
                    norms = (norms[1], norms[0] + held * held)
            return norms

        norms = lax.fori_loop(0, 3 * T // BUNROLL, block, (zero, zero))
        return total(norms[0] + norms[1]) if norm else None

    even, odd = searches
    product, norm = apply(None, even, None, first=True)
    step = wide(norm / product)
    norm_next = update(step, even, [(step, even)], add=False)

    def pair(_, carry):
        norm, norm_next = carry
        product, _ = apply(even, odd, wide(norm_next / norm))
        first_step = wide(norm_next / product)
        norm, norm_next = norm_next, update(first_step, resid, [])
        product, _ = apply(odd, even, wide(norm_next / norm))
        step = wide(norm_next / product)
        return norm_next, update(step, resid, [(first_step, odd), (step, even)])

    norm, norm_next = lax.fori_loop(0, (ITERS - 2) // 2, pair, (norm, norm_next))
    product, _ = apply(even, odd, wide(norm_next / norm), last=True)
    update(None, None, [(wide(norm_next / product), odd)], norm=False)


def solve_kernel(
    base_in, weight_in, wall, products, jumps, lifts, lines_in, columns,
    out, own_disp,
    disp, resid, search_a, search_b, image, diag, picked, flux, lines, base, weight, in_sem,
):
    pairs = [(lines_in, lines), (base_in, base), (weight_in, weight)]
    local = [pltpu.make_async_copy(a, b, in_sem.at[i]) for i, (a, b) in enumerate(pairs)]
    for copy in local:
        copy.start()
    solve_wall(wall, disp, resid, (search_a, search_b), image, diag)
    for copy in local:
        copy.wait()
    sec, dom = lax.axis_index("sec"), lax.axis_index("dom")
    line = (sec % NC) * NY + sec // NC
    for c in range(3):
        for i in range(8):
            own_disp[c, pl.ds(i, 1), :] = disp[pl.ds((c * T + dom * 8 + i) * 8 + line, 1), :]

    def pick(e, carry):
        at = lines[0, e]
        for c in range(3):
            picked[c, pl.ds(e, 1), :] = disp[pl.ds(c * T * 8 + at, 1), :]
        return carry

    lax.fori_loop(0, NE, pick, 0, unroll=32)
    geometry = []
    for k in range(4):
        row = base[pl.ds(k, 1), :]
        if k < 3:
            found = []
            for start in range(0, NE, 128):
                turned = jnp.transpose(picked[k, pl.ds(start, 128), :])
                chosen = jnp.where(columns[:, pl.ds(start, 128)] != 0.0, turned, 0.0)
                found.append(jnp.sum(chosen, axis=0, keepdims=True))
            row = row * jnp.exp(weight[...] * jnp.concatenate(found, axis=1))
        geometry.append(row)
    for face in range(6):
        at = pl.ds(face * 128, 128)
        flux[at, :] = (geometry[face // 2] * jumps[at, :]).astype(BF16)
    result = dot(lifts[...], flux[...])
    for k in range(4):
        result = result + geometry[k] * products[k]
    out[...] = result.astype(BF16)


def on_device(
    flow_state, base_geometry, anchor_weight, wall_anchor, face_nbr, volume_ops, lift_ops, face_jac, wall_load, wall_stiff
):
    wall, *prepared = exchange(
        wall_load, wall_stiff, flow_state, face_nbr, wall_anchor, volume_ops, lift_ops, face_jac
    )
    wall = wall.reshape(3 * T * 9, 128)
    vmem = pl.BlockSpec(memory_space=pltpu.VMEM)
    far = pl.BlockSpec(memory_space=pltpu.HBM)
    field = pltpu.VMEM((3 * T * 8, 128), F32)
    return pl.pallas_call(
        solve_kernel,
        out_shape=(
            jax.ShapeDtypeStruct((NQ, NE), BF16),
            jax.ShapeDtypeStruct((3, 8, 128), F32),
        ),
        in_specs=[far] * 2 + [vmem] * 6,
        out_specs=(vmem, vmem),
        scratch_shapes=[field] * 6
        + [
            pltpu.VMEM((3, NE, 128), F32),
            pltpu.VMEM((768, NE), BF16),
            pltpu.SMEM((1, NE), jnp.int32),
            pltpu.VMEM((4, NE), F32),
            pltpu.VMEM((1, NE), F32),
            pltpu.SemaphoreType.DMA((3,)),
        ],
        compiler_params=pltpu.CompilerParams(vmem_limit_bytes=28 << 20),
        name="solve",
    )(
        *map(stay, (base_geometry, anchor_weight.reshape(1, NE))), wall, *prepared
    )


def solution(mesh):
    return jax.shard_map(
        on_device,
        mesh=mesh,
        in_specs=(
            P(None, ("sec", "dom")),
            P(None, ("sec", "dom")),
            P(("sec", "dom")),
            P(("sec", "dom")),
            P(None, ("sec", "dom")),
            P(),
            P(),
            P(),
            P(None, ("sec", "dom"), None),
            P(None, ("sec", "dom"), None),
        ),
        out_specs=(P(None, ("sec", "dom")), P(None, ("sec", "dom"), None)),
        check_vma=False,
    )
```
